32 devices in a mesh: seq: 8 (over y, x, core), tp: 4 (over z).
Axes of the slice: x: 2, y: 2, z: 4, core: 2. Of those that a mesh axis runs over, the one named last changes fastest.
Arguments:
- hidden_in: bfloat16 [8192, 2048], P('seq', 'tp'), may hold values from -6 to 6
- segment_ids: int32 [8192], P('seq'), may hold values from 0 to 7, never falling along the last dimension, each value on 1 to 4096 neighbouring positions
- first_gain: float32 [2048], replicated, may hold values from 0.5 to 1.5
- input_weight: bfloat16 [2048, 2816], P(None, 'tp'), may hold values from -0.125 to 0.125
- gelu_weight: bfloat16 [2048, 2816], P(None, 'tp'), may hold values from -0.125 to 0.125
- conv_weight: float32 [4, 2816], P(None, 'tp'), may hold values from -3 to 3
- conv_bias: float32 [2816], P('tp'), may hold values from -3 to 3
- recur_gate: bfloat16 [16, 176, 176], P('tp'), may hold values from -0.4375 to 0.4375
- input_gate: bfloat16 [16, 176, 176], P('tp'), may hold values from -0.4375 to 0.4375
- recur_bias: float32 [2816], P('tp'), may hold values from -4 to 4
- input_bias: float32 [2816], P('tp'), may hold values from -4 to 4
- decay_param: float32 [2816], P('tp'), may hold values from 5 to 15
- output_weight: bfloat16 [2816, 2048], P('tp'), may hold values from -0.3125 to 0.3125
- second_gain: float32 [2048], replicated, may hold values from 0.5 to 1.5
- gate_weight: bfloat16 [2048, 6144], P('seq', 'tp'), may hold values from -0.125 to 0.125
- up_weight: bfloat16 [2048, 6144], P('seq', 'tp'), may hold values from -0.125 to 0.125
- down_weight: bfloat16 [6144, 2048], P('tp', 'seq'), may hold values from -0.109375 to 0.109375
- grad_out: bfloat16 [8192, 2048], P('seq'), may hold values from -6 to 6
Outputs:
- block_out: bfloat16 [8192, 2048], P('seq', 'tp')
- grad_in: bfloat16 [8192, 2048], P('seq', 'tp')
- grad_first_gain: float32 [2048], replicated
- grad_input_weight: float32 [2048, 2816], P(None, 'tp')
- grad_gelu_weight: float32 [2048, 2816], P(None, 'tp')
- grad_conv_weight: float32 [4, 2816], P(None, 'tp')
- grad_conv_bias: float32 [2816], P('tp')
- grad_recur_gate: float32 [16, 176, 176], P('tp')
- grad_input_gate: float32 [16, 176, 176], P('tp')
- grad_recur_bias: float32 [2816], P('tp')
- grad_input_bias: float32 [2816], P('tp')
- grad_decay: float32 [2816], P('tp')
- grad_output_weight: float32 [2816, 2048], P('tp')
- grad_second_gain: float32 [2048], replicated
- grad_gate_weight: float32 [2048, 6144], P('seq', 'tp')
- grad_up_weight: float32 [2048, 6144], P('seq', 'tp')
- grad_down_weight: float32 [6144, 2048], P('tp', 'seq')
- final_states: float32 [8, 2816], P(None, 'tp')
The draws below stay inside these ranges and needn't reach their ends.
Inputs may be any that keep to these rules, and one draw needn't show every extreme that they name: `segment_ids`: Non-decreasing along the stream; every segment number occurs; each segment has 1 to 4096 tokens and one has exactly 4096.
All inputs are finite; a program needn't handle non-finite values.
Results may differ from the reference program's by a relative error of at most 0.009.
Values may be sent and summed in bfloat16 or wider, within the bound.
No kernel may reach another device: no remote copies, remote signals or barrier semaphores. Data moves between devices by JAX's collectives and lax.ppermute only.
A program may use at most 448 MiB of HBM per device.

```python
import math
import jax
import jax.numpy as jnp
import numpy as np
from jax import lax

D = 2048
R = 2816
BLOCKS = 16
BLOCK = 176
FF = 6144
CONV = 4
SEGS = 8
TOKENS = 8192
LONGEST = 4096


def with_spikes(values, stream_key, source, target, parts, factor):
    def block_of(axis_at):
        return (jnp.arange(values.shape[axis_at]) // (values.shape[axis_at] // parts)).reshape((-1,) + (1,) * (values.ndim - 1 - axis_at))

    first = jax.random.permutation(stream_key, parts)[block_of(target)]
    second = (block_of(target) + parts // 2) % parts
    return jnp.where((block_of(source) == first) | (block_of(source) == second), factor * values, values)


def steps_of(stream_key, extent, shards, smallest, largest):
    loudness, own = 1.0, jax.random.fold_in(stream_key, 6)
    for axis_at, shards_of in shards:
        draws = jnp.exp(jax.random.uniform(jax.random.fold_in(own, axis_at), (shards_of,), jnp.float32, smallest / len(shards), largest / len(shards)))
        loudness = loudness * jnp.repeat(draws, extent[axis_at] // shards_of).reshape([-1 if axis == axis_at else 1 for axis in range(len(extent))])
    return loudness


def profile(number_of, total, most, skew):
    portions = [(1 << 20) // math.isqrt(rank ** skew) + 1 for rank in range(2, number_of + 1)]
    rest, holding = total - most - (number_of - 1), [1] * (number_of - 1)
    while rest > 0:
        candidates = [i for i in range(number_of - 1) if holding[i] < most]
        whole, remaining = sum([portions[i] for i in candidates]), rest
        for i in candidates:
            more = min(most - holding[i], max(1, remaining * portions[i] // whole), rest)
            holding[i] = holding[i] + more
            rest = rest - more
    return np.array([most] + holding)


def ragged_sizes(rng, count, total, most, lean):
    if count == 2:
        one = jax.random.randint(rng, (), max(1, total - most), min(most, total - 1) + 1)
        return jnp.stack([one, total - one])
    lengths = jnp.asarray(profile(count, total, most, lean), jnp.int32)
    twos = (count - 1) // 2
    giver, sink = lengths[1:1 + 2 * twos:2], lengths[2:2 + 2 * twos:2]
    room = jnp.minimum(giver - 1, most - sink)
    passed = jax.random.randint(jax.random.fold_in(rng, 1), (twos,), 0, 1 << 20) % (room + 1)
    lengths = lengths.at[1:1 + 2 * twos:2].set(giver - passed).at[2:2 + 2 * twos:2].set(sink + passed)
    return lengths[jax.random.permutation(jax.random.fold_in(rng, 2), count)]


def gaussian(own_key, dims, width, limit, split=(), held_as=jnp.bfloat16):
    loudness = steps_of(own_key, dims, split, -0.22, 0.18) if split else 1.0
    array = jax.random.normal(own_key, dims, jnp.float32) * width * loudness
    return jnp.minimum(jnp.maximum(array, -limit), limit).astype(held_as)


def noise_with(own_key, extent, deviation, limit, shards, heavy, kind=jnp.bfloat16):
    drawn = deviation * jax.random.normal(own_key, extent, jnp.float32)
    if shards:
        drawn = drawn * steps_of(own_key, extent, shards, -0.22, 0.18)
    return jnp.clip(with_spikes(drawn, jax.random.fold_in(own_key, 3), *heavy), -limit, limit).astype(kind)


def setup_inputs(seed: int = 0) -> dict:
    keys = jax.random.split(jax.random.key(seed), 19)
    return {
        "hidden_in": gaussian(keys[0], (TOKENS, D), 1.0, 6.0, ((0, 8), (1, 4))),
        "segment_ids": jnp.searchsorted(jnp.cumsum(ragged_sizes(keys[1], SEGS, TOKENS, LONGEST, 0)), jnp.arange(TOKENS), side="right").astype(jnp.int32),
        "first_gain": jnp.clip(1.0 + 0.1 * jax.random.normal(keys[2], (D,), jnp.float32), 0.5, 1.5),
        "input_weight": gaussian(keys[3], (D, R), D ** -0.5, 0.125, ((1, 4),)),
        "gelu_weight": gaussian(keys[4], (D, R), D ** -0.5, 0.125, ((1, 4),)),
        "conv_weight": gaussian(keys[5], (CONV, R), CONV ** -0.5, 3.0, ((1, 4),), jnp.float32),
        "conv_bias": gaussian(keys[6], (R,), 0.5, 3.0, ((0, 4),), jnp.float32),
        "recur_gate": gaussian(keys[7], (BLOCKS, BLOCK, BLOCK), BLOCK ** -0.5, 0.4375, ((0, 4),)),
        "input_gate": gaussian(keys[8], (BLOCKS, BLOCK, BLOCK), BLOCK ** -0.5, 0.4375, ((0, 4),)),
        "recur_bias": gaussian(keys[9], (R,), 1.0, 4.0, ((0, 4),), jnp.float32),
        "input_bias": gaussian(keys[10], (R,), 1.0, 4.0, ((0, 4),), jnp.float32),
        "decay_param": jnp.clip(5.0 + 10.0 * jax.random.uniform(keys[11], (R,), jnp.float32) ** steps_of(keys[11], (R,), ((0, 4),), -0.2, 0.2), 5.0, 15.0),
        "output_weight": gaussian(keys[12], (R, D), (R // 8) ** -0.5, 0.3125, ((0, 4),)),
        "second_gain": jnp.clip(1.0 + 0.1 * jax.random.normal(keys[13], (D,), jnp.float32), 0.5, 1.5),
        "gate_weight": gaussian(keys[14], (D, FF), D ** -0.5, 0.125, ((0, 8), (1, 4))),
        "up_weight": gaussian(keys[15], (D, FF), D ** -0.5, 0.125, ((0, 8), (1, 4))),
        "down_weight": gaussian(keys[16], (FF, D), (FF // 2) ** -0.5, 0.109375, ((0, 4), (1, 8))),
        "grad_out": noise_with(keys[17], (TOKENS, D), 1.0, 6.0, ((0, 8),), (0, 1, 8, 2.0)),
    }


@jax.custom_vjp
def low(v):
    return lax.optimization_barrier(v.astype(jnp.bfloat16)).astype(jnp.float32)

@jax.custom_vjp
def low_back(v):
    return v

def low_keep(v):
    return (low(v), None)

def low_pass(kept, grad):
    return (grad,)

def back_keep(v):
    return (v, None)

def back_low(kept, grad):
    return (low(grad),)
low.defvjp(low_keep, low_pass)
low_back.defvjp(back_keep, back_low)
EPSILON = 1e-06
DECAY_SCALE = 8.0

def matmul(left, right):
    return jnp.dot(left, right, precision=lax.Precision.HIGHEST)

def rms_norm(value, gain):
    return value * lax.rsqrt(lax.optimization_barrier(jnp.mean(value * value, axis=1, keepdims=True)) + EPSILON) * gain

def shifted(value, offset, fill):
    head = jnp.full((offset,) + value.shape[1:], fill, value.dtype)
    return jnp.concatenate([head, value[:value.shape[0] - offset]], axis=0)

def reference(hidden_in, segment_ids, first_gain, input_weight, gelu_weight, conv_weight, conv_bias, recur_gate, input_gate, recur_bias, input_bias, decay_param, output_weight, second_gain, gate_weight, up_weight, down_weight, grad_out):
    ids = segment_ids.astype(jnp.int32)
    prev_ids = shifted(ids, 1, -1)
    next_ids = jnp.concatenate([ids[1:], jnp.full((1,), -1, jnp.int32)])
    restart = (prev_ids != ids)[:, None]
    masks = [(shifted(ids, offset, -1) == ids).astype(jnp.float32)[:, None] for offset in range(CONV)]
    ends = (next_ids != ids).astype(jnp.float32)[:, None]
    member = (ids[:, None] == jnp.arange(SEGS, dtype=jnp.int32)[None, :]).astype(jnp.float32)

    def forward(block_in, gain_first, weight_in, weight_gelu, conv_taps, conv_shift, recur_mat, input_mat, recur_off, input_off, decay_value, weight_out, gain_second, weight_gate, weight_up, weight_down):
        normed = low(rms_norm(block_in, gain_first))
        branch_x = low_back(matmul(normed, weight_in))
        branch_y = low_back(matmul(normed, weight_gelu))
        conv_out = conv_shift + sum((conv_taps[offset] * shifted(branch_x, offset, 0.0) * masks[offset] for offset in range(CONV)))
        conv_low = low(conv_out).reshape(TOKENS, BLOCKS, BLOCK)
        pre_recur = low_back(jnp.einsum('tbi,bij->tbj', conv_low, recur_mat, precision=lax.Precision.HIGHEST).reshape(TOKENS, R))
        pre_input = low_back(jnp.einsum('tbi,bij->tbj', conv_low, input_mat, precision=lax.Precision.HIGHEST).reshape(TOKENS, R))
        rate_gate = jax.nn.sigmoid(pre_recur + recur_off)
        in_gate = jax.nn.sigmoid(pre_input + input_off)
        log_decay = -DECAY_SCALE * rate_gate * jax.nn.softplus(-decay_value)
        carried = jnp.where(restart, 0.0, jnp.exp(log_decay))
        scaled = jnp.where(restart, 1.0, jnp.sqrt(-jnp.expm1(2.0 * log_decay)))
        drive = scaled * in_gate * conv_out

        def advance(carry_state, inputs):
            new_state = inputs[0] * carry_state + inputs[1]
            return (new_state, new_state)
        last_state, states = lax.scan(advance, jnp.zeros((R,), jnp.float32), (carried, drive))
        mixed = low(jax.nn.gelu(branch_y) * states)
        resid = block_in + low_back(matmul(mixed, weight_out))
        normed2 = low(rms_norm(resid, gain_second))
        gate_pre = low_back(matmul(normed2, weight_gate))
        up_pre = low_back(matmul(normed2, weight_up))
        hid = low(jax.nn.gelu(gate_pre) * up_pre)
        finals = matmul(member.T, states * ends)
        return (resid + low_back(matmul(hid, weight_down)), finals)
    primals = (hidden_in.astype(jnp.float32), first_gain, input_weight.astype(jnp.float32), gelu_weight.astype(jnp.float32), conv_weight, conv_bias, recur_gate.astype(jnp.float32), input_gate.astype(jnp.float32), recur_bias, input_bias, decay_param, output_weight.astype(jnp.float32), second_gain, gate_weight.astype(jnp.float32), up_weight.astype(jnp.float32), down_weight.astype(jnp.float32))
    (block_out, final_states), pullback = jax.vjp(forward, *primals)
    grads = pullback((grad_out.astype(jnp.float32), jnp.zeros_like(final_states)))
    return (block_out.astype(jnp.bfloat16), grads[0].astype(jnp.bfloat16), grads[1], grads[2], grads[3], grads[4], grads[5], grads[6], grads[7], grads[8], grads[9], grads[10], grads[11], grads[12], grads[13], grads[14], grads[15], final_states)
```

```python
import functools

import jax
import jax.numpy as jnp
from jax import lax
from jax.experimental import pallas as pl
from jax.experimental.pallas import tpu as pltpu
from jax.sharding import PartitionSpec as P

SEGS = 8
EPSILON = 1e-06
DECAY_SCALE = 8.0
GELU_C = 0.7978845608028654
GELU_A = 0.044715
F32 = jnp.float32
BF16 = jnp.bfloat16
VMEM_LIMIT = 48 << 20


def shifted(x, axis, by):
    peers = lax.axis_size(axis)
    pairs = [(i, i + by) for i in range(peers) if 0 <= i + by < peers]
    return lax.ppermute(x, axis, pairs)


def dot(left, right):
    return jnp.dot(left, right, preferred_element_type=F32)


def contract_first(left, right):
    return lax.dot_general(left, right, (((0,), (0,)), ((), ())), preferred_element_type=F32)


def contract_last(left, right):
    return lax.dot_general(left, right, (((1,), (1,)), ((), ())), preferred_element_type=F32)


def gelu_parts(y):
    y2 = y * y
    t = jnp.tanh(GELU_C * y * (1.0 + GELU_A * y2))
    half = 0.5 * (1.0 + t)
    slope = half + 0.5 * y * (1.0 - t * t) * (GELU_C * (1.0 + 3.0 * GELU_A * y2))
    return y * half, slope


def gelu(y):
    return y * (0.5 * (1.0 + jnp.tanh(GELU_C * y * (1.0 + GELU_A * y * y))))


def retained(log_decay, carried):
    y = 2.0 * log_decay
    series = -y * (
        1.0
        + y
        * (1 / 2 + y * (1 / 6 + y * (1 / 24 + y * (1 / 120 + y * (1 / 720 + y * (1 / 5040))))))
    )
    return jnp.maximum(jnp.where(y > -0.25, series, 1.0 - carried * carried), 1e-36)


def block_scan(a, b, reverse):
    row = lax.broadcasted_iota(jnp.int32, a.shape, 0)
    for s in (1, 2, 4):
        by = 8 - s if reverse else s
        live = row < 8 - s if reverse else row >= s
        b_shift = pltpu.roll(b, by, 0)
        a_shift = pltpu.roll(a, by, 0)
        b = b + a * jnp.where(live, b_shift, 0.0)
        a = a * jnp.where(live, a_shift, 1.0)
    return a, b


def forward_kernel(
    bx_ref, prev_ref, mask_ref, par_ref, gates_ref,
    conv_ref, low_ref, r_ref, i_ref, state_ref, decay_ref,
    window, pre, carry,
):
    rows, width = bx_ref.shape
    tile = pl.program_id(0)

    @pl.when(tile == 0)
    def _():
        window[pl.ds(0, 8), :] = prev_ref[...]
        carry[pl.ds(0, 8), :] = jnp.zeros((8, width), F32)
        carry[pl.ds(8, 8), :] = jnp.ones((8, width), F32)

    @pl.when(tile > 0)
    def _():
        window[pl.ds(0, 8), :] = window[pl.ds(rows, 8), :]

    window[pl.ds(8, rows), :] = bx_ref[...]

    def conv_step(j, _):
        at = pl.multiple_of(j * 16, 16)
        win = window[pl.ds(at, 24), :]
        mask = mask_ref[pl.ds(at, 16), :]
        out = par_ref[pl.ds(0, 1), :] + par_ref[pl.ds(1, 1), :] * win[8:24]
        for k in range(1, 4):
            out = out + par_ref[pl.ds(1 + k, 1), :] * (win[8 - k : 24 - k] * mask[:, k : k + 1])
        conv_ref[pl.ds(at, 16), :] = out
        low_ref[pl.ds(at, 16), :] = out.astype(BF16)
        return 0

    lax.fori_loop(0, rows // 16, conv_step, 0)
    pre[...] = dot(low_ref[...], gates_ref[...])

    def scan_step(j, _):
        at = pl.multiple_of(j * 8, 8)
        here = pl.ds(at, 8)
        keep = mask_ref[here, :][:, 1:2]
        r = jax.nn.sigmoid(pre[here, pl.ds(0, width)] + par_ref[pl.ds(5, 1), :])
        i = jax.nn.sigmoid(pre[here, pl.ds(width, width)] + par_ref[pl.ds(6, 1), :])
        log_decay = par_ref[pl.ds(7, 1), :] * r
        a = jnp.exp(log_decay)
        e = retained(log_decay, a)
        s = e * lax.rsqrt(e)
        r_ref[here, :] = r
        i_ref[here, :] = i
        whole = jnp.broadcast_to(keep, a.shape) != 0.0
        b = jnp.where(whole, s, 1.0) * (i * conv_ref[here, :])
        a = jnp.where(whole, a, 0.0)
        a, b = block_scan(a, b, False)
        state = b + a * carry[pl.ds(0, 8), :]
        decay = a * carry[pl.ds(8, 8), :]
        state_ref[here, :] = state
        decay_ref[here, :] = decay
        carry[pl.ds(0, 8), :] = jnp.broadcast_to(state[7:8], state.shape)
        carry[pl.ds(8, 8), :] = jnp.broadcast_to(decay[7:8], state.shape)
        return 0

    lax.fori_loop(0, rows // 8, scan_step, 0)


def forward_recurrence(bx, prev_rows, masks, params, gates):
    tokens, width = bx.shape
    rows = min(128, tokens)
    wide = pl.BlockSpec((rows, width), lambda t: (t, 0))
    whole = lambda a: pl.BlockSpec(a.shape, lambda t: (0,) * a.ndim)
    shape = lambda d: jax.ShapeDtypeStruct((tokens, width), d)
    return pl.pallas_call(
        forward_kernel,
        name="forward_recurrence",
        grid=(tokens // rows,),
        in_specs=[
            wide, whole(prev_rows), pl.BlockSpec((rows, 8), lambda t: (t, 0)), whole(params),
            whole(gates),
        ],
        out_specs=[wide] * 6,
        out_shape=[shape(F32), shape(BF16), shape(F32), shape(F32), shape(F32), shape(F32)],
        scratch_shapes=[
            pltpu.VMEM((rows + 8, width), F32),
            pltpu.VMEM((rows, 2 * width), F32),
            pltpu.VMEM((16, width), F32),
        ],
        compiler_params=pltpu.CompilerParams(
            dimension_semantics=("arbitrary",), vmem_limit_bytes=VMEM_LIMIT
        ),
        cost_estimate=pl.CostEstimate(
            flops=4 * tokens * width * width, bytes_accessed=30 * tokens * width,
            transcendentals=6 * tokens * width,
        ),
    )(bx, prev_rows, masks, params, gates)


def reverse_kernel(
    dm_ref, by_ref, r_ref, state_ref, mask_ref, par_ref,
    grad_ref, reach_ref, dby_ref, head_ref, carry,
):
    rows, width = dm_ref.shape

    @pl.when(pl.program_id(0) == 0)
    def _():
        carry[pl.ds(0, 8), :] = jnp.zeros((8, width), F32)
        carry[pl.ds(8, 8), :] = jnp.ones((8, width), F32)

    groups = rows // 16

    def step(j, _):
        base = pl.multiple_of((groups - 1 - j) * 16, 16)
        slopes = []
        for half in (1, 0):
            at = pl.multiple_of(base + 8 * half, 8)
            here = pl.ds(at, 8)
            dm = dm_ref[here, :]
            act, slope = gelu_parts(by_ref[here, :])
            slopes.append(slope * (state_ref[here, :] * dm))
            keep = mask_ref[here, :][:, 1:2]
            a = jnp.exp(par_ref[pl.ds(7, 1), :] * r_ref[here, :])
            a = jnp.where(jnp.broadcast_to(keep, a.shape) != 0.0, a, 0.0)
            dh = dm * act
            acc, u = block_scan(a, a * dh, True)
            u_next = carry[pl.ds(0, 8), :]
            reach_next = carry[pl.ds(8, 8), :]
            u = u + acc * u_next
            reach = acc * reach_next
            last = lax.broadcasted_iota(jnp.int32, u.shape, 0) == 7
            grad_ref[here, :] = dh + jnp.where(last, u_next, pltpu.roll(u, 7, 0))
            reach_ref[here, :] = jnp.where(last, reach_next, pltpu.roll(reach, 7, 0))
            carry[pl.ds(0, 8), :] = jnp.broadcast_to(u[0:1], u.shape)
            carry[pl.ds(8, 8), :] = jnp.broadcast_to(reach[0:1], u.shape)
        dby_ref[pl.ds(base, 16), :] = jnp.concatenate(slopes[::-1], axis=0).astype(BF16)
        return 0

    lax.fori_loop(0, groups, step, 0)
    head_ref[...] = carry[...]


def reverse_recurrence(dm, by, r, state, masks, params):
    tokens, width = dm.shape
    rows = min(128, tokens)
    tiles = tokens // rows
    wide = pl.BlockSpec((rows, width), lambda t: (tiles - 1 - t, 0))
    whole = lambda a: pl.BlockSpec(a.shape, lambda t: (0,) * a.ndim)
    shape = lambda d: jax.ShapeDtypeStruct((tokens, width), d)
    return pl.pallas_call(
        reverse_kernel,
        name="reverse_recurrence",
        grid=(tiles,),
        in_specs=[
            wide, wide, wide, wide, pl.BlockSpec((rows, 8), lambda t: (tiles - 1 - t, 0)),
            whole(params),
        ],
        out_specs=[wide, wide, wide, pl.BlockSpec((16, width), lambda t: (0, 0))],
        out_shape=[shape(F32), shape(F32), shape(BF16), jax.ShapeDtypeStruct((16, width), F32)],
        scratch_shapes=[pltpu.VMEM((16, width), F32)],
        compiler_params=pltpu.CompilerParams(
            dimension_semantics=("arbitrary",), vmem_limit_bytes=VMEM_LIMIT
        ),
        cost_estimate=pl.CostEstimate(
            flops=60 * tokens * width, bytes_accessed=28 * tokens * width,
            transcendentals=2 * tokens * width,
        ),
    )(dm, by, r, state, masks, params)


def gate_grad_kernel(
    grad_ref, reach_ref, r_ref, i_ref, conv_ref, state_ref, before_ref, bx_ref, bx_before_ref,
    mask_ref, low_ref, prev_ref, ends_ref, par_ref, gates_ref,
    dbx_ref, tail_ref, edge_ref, sums_ref, gate_ref,
    window, states, pair, direct, spread,
):
    rows, width = grad_ref.shape
    step_at = pl.program_id(0)
    tiles = pl.num_programs(0)
    first = step_at == tiles - 1

    @pl.when(step_at == 0)
    def _():
        sums_ref[...] = jnp.zeros_like(sums_ref)
        spread[...] = jnp.zeros_like(spread)

    @pl.when(first)
    def _():
        window[pl.ds(0, 8), :] = prev_ref[...]
        states[pl.ds(0, 8), :] = jnp.broadcast_to(ends_ref[pl.ds(0, 1), :], (8, width))

    @pl.when(jnp.logical_not(first))
    def _():
        window[pl.ds(0, 8), :] = bx_before_ref[...]
        states[pl.ds(0, 8), :] = before_ref[...]

    window[pl.ds(8, rows), :] = bx_ref[...]
    states[pl.ds(8, rows), :] = state_ref[...]

    def gates_step(j, sums):
        sum_r, sum_i, sum_d = sums
        at = pl.multiple_of(j * 16, 16)
        outs = []
        for half in (0, 1):
            off = pl.multiple_of(at + 8 * half, 8)
            here = pl.ds(off, 8)
            grad = grad_ref[here, :] + reach_ref[here, :] * ends_ref[pl.ds(1, 1), :]
            r, i = r_ref[here, :], i_ref[here, :]
            conv = conv_ref[here, :]
            keep = jnp.broadcast_to(mask_ref[here, :][:, 1:2], grad.shape) != 0.0
            log_decay = par_ref[pl.ds(7, 1), :] * r
            a = jnp.exp(log_decay)
            e = retained(log_decay, a)
            inv = lax.rsqrt(e)
            s = jnp.where(keep, e * inv, 1.0)
            states_win = states[pl.ds(off, 16), :]
            before = states_win[7:15]
            gi = grad * i
            d_log = jnp.where(keep, a * (grad * before - gi * conv * a * inv), 0.0)
            d_pa = d_log * par_ref[pl.ds(7, 1), :] * r * (1.0 - r)
            gs = gi * s
            d_pi = gs * conv * (1.0 - i)
            direct[here, :] = gs
            sum_r = sum_r + d_pa
            sum_i = sum_i + d_pi
            sum_d = sum_d + d_log * r
            outs.append((d_pa, d_pi))
        pair[pl.ds(at, 16), pl.ds(0, width)] = jnp.concatenate([o[0] for o in outs], 0).astype(BF16)
        pair[pl.ds(at, 16), pl.ds(width, width)] = jnp.concatenate([o[1] for o in outs], 0).astype(BF16)
        return sum_r, sum_i, sum_d

    zero = jnp.zeros((8, width), F32)
    sum_r, sum_i, sum_d = lax.fori_loop(0, rows // 16, gates_step, (zero, zero, zero))
    for n, total in enumerate((sum_r, sum_i, sum_d)):
        sums_ref[pl.ds(8 * n, 8), :] += total

    part = contract_first(low_ref[...], pair[...])

    @pl.when(step_at == 0)
    def _():
        gate_ref[...] = part

    @pl.when(step_at > 0)
    def _():
        gate_ref[...] += part

    direct[...] += contract_last(pair[...], gates_ref[...])

    for k in range(1, 4):
        spread[k - 1, pl.ds(rows, 8), :] = spread[k - 1, pl.ds(0, 8), :]

    def conv_step(j, sums):
        at = pl.multiple_of(j * 8, 8)
        here = pl.ds(at, 8)
        d_conv = direct[here, :]
        mask = mask_ref[here, :]
        win = window[pl.ds(at, 16), :]
        out = [sums[0] + d_conv, sums[1] + d_conv * win[8:16]]
        for k in range(1, 4):
            masked = d_conv * mask[:, k : k + 1]
            spread[k - 1, here, :] = masked
            out.append(sums[k + 1] + masked * win[8 - k : 16 - k])
        return tuple(out)

    totals = lax.fori_loop(0, rows // 8, conv_step, (zero,) * 5)
    for n, total in enumerate(totals):
        sums_ref[pl.ds(24 + 8 * n, 8), :] += total

    def back_step(j, _):
        at = pl.multiple_of(j * 16, 16)
        out = par_ref[pl.ds(1, 1), :] * direct[pl.ds(at, 16), :]
        for k in range(1, 4):
            win = spread[k - 1, pl.ds(at, 24), :]
            out = out + par_ref[pl.ds(1 + k, 1), :] * win[k : 16 + k]
        direct[pl.ds(at, 16), :] = out
        dbx_ref[pl.ds(at, 16), :] = out.astype(BF16)
        return 0

    lax.fori_loop(0, rows // 16, back_step, 0)

    @pl.when(step_at == 0)
    def _():
        tail_ref[...] = direct[pl.ds(rows - 8, 8), :]

    @pl.when(first)
    def _():
        row = lax.broadcasted_iota(jnp.int32, (8, width), 0)
        edge = jnp.zeros((8, width), F32)
        for k in range(1, 4):
            head = pltpu.roll(spread[k - 1, pl.ds(0, 8), :], 8 - k, 0)
            edge = edge + par_ref[pl.ds(1 + k, 1), :] * jnp.where(row >= 8 - k, head, 0.0)
        edge_ref[...] = edge


def gate_gradients(grad, reach, r, i, conv, state, bx, masks, low, prev_rows, ends, params, gates):
    tokens, width = grad.shape
    rows = min(128, tokens)
    tiles = tokens // rows
    wide = pl.BlockSpec((rows, width), lambda t: (tiles - 1 - t, 0))
    before = pl.BlockSpec(
        (8, width), lambda t: (jnp.maximum((tiles - 1 - t) * (rows // 8) - 1, 0), 0)
    )
    whole = lambda a: pl.BlockSpec(a.shape, lambda t: (0,) * a.ndim)
    fixed = lambda *dims: pl.BlockSpec(dims, lambda t: (0,) * len(dims))
    return pl.pallas_call(
        gate_grad_kernel,
        name="gate_gradients",
        grid=(tiles,),
        in_specs=[
            wide, wide, wide, wide, wide, wide, before, wide, before,
            pl.BlockSpec((rows, 8), lambda t: (tiles - 1 - t, 0)), wide, whole(prev_rows),
            whole(ends), whole(params), whole(gates),
        ],
        out_specs=[
            wide, fixed(8, width), fixed(8, width), fixed(64, width), fixed(width, 2 * width),
        ],
        out_shape=[
            jax.ShapeDtypeStruct((tokens, width), BF16),
            jax.ShapeDtypeStruct((8, width), F32),
            jax.ShapeDtypeStruct((8, width), F32),
            jax.ShapeDtypeStruct((64, width), F32),
            jax.ShapeDtypeStruct((width, 2 * width), F32),
        ],
        scratch_shapes=[
            pltpu.VMEM((rows + 8, width), F32),
            pltpu.VMEM((rows + 8, width), F32),
            pltpu.VMEM((rows, 2 * width), BF16),
            pltpu.VMEM((rows, width), F32),
            pltpu.VMEM((3, rows + 8, width), F32),
        ],
        compiler_params=pltpu.CompilerParams(
            dimension_semantics=("arbitrary",), vmem_limit_bytes=VMEM_LIMIT
        ),
        cost_estimate=pl.CostEstimate(
            flops=8 * tokens * width * width, bytes_accessed=32 * tokens * width,
            transcendentals=2 * tokens * width,
        ),
    )(grad, reach, r, i, conv, state, state, bx, bx, masks, low, prev_rows, ends, params, gates)


def chained(decays, values, place, reverse):
    count = decays.shape[0]
    total = jnp.zeros_like(values[0])
    for hop in range(count - 1):
        source = count - 1 - hop if reverse else hop
        live = source > place if reverse else source < place
        total = jnp.where(live, values[source] + decays[source] * total, total)
    return total


def block_diagonal(blocks):
    count, size, _ = blocks.shape
    rows = [
        jnp.pad(blocks[b], ((0, 0), (b * size, (count - 1 - b) * size))) for b in range(count)
    ]
    return jnp.concatenate(rows, axis=0)


def on_device(
    hidden_in, segment_ids, first_gain, input_weight, gelu_weight, conv_weight, conv_bias,
    recur_gate, input_gate, recur_bias, input_bias, decay_param, output_weight, second_gain,
    gate_weight, up_weight, down_weight, grad_out,
):
    tokens, share = hidden_in.shape
    channels = input_weight.shape[1]
    taps = conv_weight.shape[0]
    halo = taps - 1
    blocks, size = recur_gate.shape[0], recur_gate.shape[1]
    width = grad_out.shape[1]
    seq_devices = lax.axis_size("seq")
    seq_place = lax.axis_index("seq")
    share_start = lax.axis_index("tp") * share

    gate_full = lax.all_gather(gate_weight, "seq", axis=0, tiled=True)
    up_full = lax.all_gather(up_weight, "seq", axis=0, tiled=True)
    down_full = lax.all_gather(down_weight, "seq", axis=1, tiled=True)

    ids = segment_ids.astype(F32)
    prev_ids = shifted(ids[tokens - halo :], "seq", 1)
    prev_ids = jnp.where(seq_place == 0, -1.0, prev_ids)
    next_id = jnp.where(seq_place == seq_devices - 1, -1.0, shifted(ids[:1], "seq", -1))
    ext = jnp.concatenate([prev_ids, ids])
    same = [(ext[halo - k : halo - k + tokens] == ids).astype(F32) for k in range(taps)]
    masks = jnp.stack(same + [jnp.zeros_like(ids)] * (8 - taps), axis=1)

    slope = -DECAY_SCALE * jax.nn.softplus(-decay_param)
    params = jnp.concatenate(
        [jnp.stack([conv_bias]), conv_weight, jnp.stack([recur_bias, input_bias, slope])], axis=0
    )
    gates = jnp.concatenate([block_diagonal(recur_gate), block_diagonal(input_gate)], axis=1)

    full = lax.all_gather(hidden_in, "tp", axis=1, tiled=True)
    x = full.astype(F32)
    r1 = lax.rsqrt(jnp.mean(x * x, axis=1, keepdims=True) + EPSILON)
    n1 = (x * r1 * first_gain).astype(BF16)
    bx = dot(n1, input_weight)
    by = dot(n1, gelu_weight)
    prev_rows = jnp.pad(shifted(bx[tokens - halo :], "seq", 1), ((8 - halo, 0), (0, 0)))
    conv, low, r, i, local, reach = forward_recurrence(bx, prev_rows, masks, params, gates)
    ends = lax.all_gather(
        jnp.stack([reach[tokens - 1], local[tokens - 1]]), "seq", axis=0
    )
    incoming = chained(ends[:, 0], ends[:, 1], seq_place, False)
    state = local + reach * incoming
    mixed = (gelu(by) * state).astype(BF16)
    branch = dot(mixed, output_weight).astype(BF16)
    x_share = hidden_in.astype(F32)
    resid = x_share + lax.psum_scatter(branch, "tp", scatter_dimension=1, tiled=True).astype(F32)

    resid_full = lax.all_gather(resid.astype(BF16), "tp", axis=1, tiled=True).astype(F32)
    r2 = lax.rsqrt(jnp.mean(resid_full * resid_full, axis=1, keepdims=True) + EPSILON)
    n2 = (resid_full * r2 * second_gain).astype(BF16)
    gate = dot(n2, gate_full)
    up = dot(n2, up_full)
    d_hid = contract_last(grad_out, down_full)
    act, act_slope = gelu_parts(gate)
    hid = (act * up).astype(BF16)
    d_gate_f = act_slope * up * d_hid
    d_up_f = act * d_hid
    d_gate = d_gate_f.astype(BF16)
    d_up = d_up_f.astype(BF16)
    mlp = dot(hid, down_full).astype(BF16)
    d_n2_part = (contract_last(d_gate, gate_full) + contract_last(d_up, up_full)).astype(BF16)
    pull2 = lax.psum(
        jnp.sum(d_gate.astype(F32) * gate + d_up.astype(F32) * up, axis=1), "tp"
    )[:, None]
    d_n2 = lax.psum_scatter(d_n2_part, "tp", scatter_dimension=1, tiled=True).astype(F32)
    grad_second = jnp.sum(d_n2 * resid * r2, axis=0)
    gain_share = lax.dynamic_slice_in_dim(second_gain, share_start, share)
    scaled = d_n2 * gain_share * r2
    centre = r2 * r2 * pull2 * (1.0 / width)
    g_share = lax.dynamic_slice_in_dim(grad_out, share_start, share, 1).astype(F32)
    d_resid_share = g_share + scaled - resid * centre
    scaled_full = lax.all_gather(scaled.astype(BF16), "tp", axis=1, tiled=True).astype(F32)
    d_resid_low = (grad_out.astype(F32) + scaled_full - resid_full * centre).astype(BF16)
    block_out = (
        resid + lax.psum_scatter(mlp, "tp", scatter_dimension=1, tiled=True).astype(F32)
    ).astype(BF16)

    grad_gate_weight = lax.psum_scatter(
        contract_first(n2, d_gate).astype(BF16), "seq", scatter_dimension=0, tiled=True
    ).astype(F32)
    grad_up_weight = lax.psum_scatter(
        contract_first(n2, d_up).astype(BF16), "seq", scatter_dimension=0, tiled=True
    ).astype(F32)
    grad_down_weight = lax.psum_scatter(
        contract_first(hid, grad_out).astype(BF16), "seq", scatter_dimension=1, tiled=True
    ).astype(F32)

    dm = contract_last(d_resid_low, output_weight)
    grad_output_weight = lax.psum(contract_first(mixed, d_resid_low).astype(BF16), "seq").astype(F32)
    grad_local, reach_back, dby, heads = reverse_recurrence(dm, by, r, state, masks, params)
    outgoing = lax.all_gather(jnp.stack([heads[8], heads[0]]), "seq", axis=0)
    message = chained(outgoing[:, 0], outgoing[:, 1], seq_place, True)
    border = jnp.pad(jnp.stack([incoming, message]), ((0, 6), (0, 0)))
    dbx_main, tail, edge, sums, gate_grads = gate_gradients(
        grad_local, reach_back, r, i, conv, state, bx, masks, low, prev_rows, border, params, gates
    )
    tail = (tail + shifted(edge, "seq", -1)).astype(BF16)
    dbx = lax.dynamic_update_slice_in_dim(dbx_main, tail, tokens - 8, 0)
    d_n1_part = (contract_last(dbx, input_weight) + contract_last(dby, gelu_weight)).astype(BF16)
    pull1 = lax.psum(
        jnp.sum(dbx.astype(F32) * bx + dby.astype(F32) * by, axis=1), "tp"
    )[:, None]
    grad_gelu_weight = lax.psum(contract_first(dby, n1).astype(BF16), "seq").astype(F32).T
    grad_input_weight = lax.psum(contract_first(dbx, n1).astype(BF16), "seq").astype(F32).T
    d_n1 = lax.psum_scatter(d_n1_part, "tp", scatter_dimension=1, tiled=True).astype(F32)
    grad_first = jnp.sum(d_n1 * x_share * r1, axis=0)
    gain1_share = lax.dynamic_slice_in_dim(first_gain, share_start, share)
    grad_in = (
        d_resid_share + d_n1 * gain1_share * r1 - x_share * (r1 * r1 * pull1 * (1.0 / width))
    ).astype(BF16)

    sums = jnp.sum(sums.reshape(8, 8, channels), axis=1)
    corner = lambda n: jnp.stack(
        [
            gate_grads[b * size : (b + 1) * size, n * channels + b * size : n * channels + (b + 1) * size]
            for b in range(blocks)
        ]
    )
    next_ids = jnp.concatenate([ids[1:], next_id])
    closing = (next_ids != ids).astype(F32)[None, :]
    member = (segment_ids[None, :] == jnp.arange(SEGS, dtype=jnp.int32)[:, None]).astype(F32)
    finals = jnp.dot(
        member * closing, state, precision=lax.Precision.HIGHEST, preferred_element_type=F32
    )
    small = lax.psum(jnp.concatenate([sums, finals], axis=0), "seq")
    recur_grads, input_grads = lax.psum((corner(0), corner(1)), "seq")
    gains = jnp.zeros((2, width), F32)
    gains = lax.dynamic_update_slice(
        gains, jnp.stack([grad_first, grad_second]), (0, share_start)
    )
    gains = lax.psum(gains, ("seq", "tp"))
    grad_decay = small[2] * (DECAY_SCALE * jax.nn.sigmoid(-decay_param))
    return (
        block_out,
        grad_in,
        gains[0],
        grad_input_weight,
        grad_gelu_weight,
        small[4:8],
        small[3],
        recur_grads,
        input_grads,
        small[0],
        small[1],
        grad_decay,
        grad_output_weight,
        gains[1],
        grad_gate_weight,
        grad_up_weight,
        grad_down_weight,
        small[8:],
    )


def solution(mesh):
    row = P("tp")
    return jax.shard_map(
        on_device,
        mesh=mesh,
        in_specs=(
            P("seq", "tp"), P("seq"), P(), P(None, "tp"), P(None, "tp"), P(None, "tp"), row,
            P("tp", None, None), P("tp", None, None), row, row, row, P("tp", None), P(),
            P("seq", "tp"), P("seq", "tp"), P("tp", "seq"), P("seq", None),
        ),
        out_specs=(
            P("seq", "tp"), P("seq", "tp"), P(), P(None, "tp"), P(None, "tp"), P(None, "tp"), row,
            P("tp", None, None), P("tp", None, None), row, row, row, P("tp", None), P(),
            P("seq", "tp"), P("seq", "tp"), P("tp", "seq"), P(None, "tp"),
        ),
        check_vma=False,
    )
```

```python
import jax
import jax.numpy as jnp
from jax import lax
from jax.experimental import pallas as pl
from jax.experimental.layout import Layout, with_layout_constraint
from jax.experimental.pallas import tpu as pltpu
from jax.sharding import PartitionSpec as P

SEGS = 8
EPSILON = 1e-06
DECAY_SCALE = 8.0
GELU_C = 0.7978845608028654
GELU_A = 0.044715
F32 = jnp.float32
BF16 = jnp.bfloat16
VMEM_LIMIT = 58 << 20
STEPS = 16
ROWS = 8 * STEPS


def dot(left, right):
    return jnp.dot(left, right, preferred_element_type=F32)


def contract_first(left, right):
    return lax.dot_general(left, right, (((0,), (0,)), ((), ())), preferred_element_type=F32)


def contract_last(left, right):
    return lax.dot_general(left, right, (((1,), (1,)), ((), ())), preferred_element_type=F32)


def gelu_parts(y):
    y2 = y * y
    t = jnp.tanh(y * (GELU_C + (GELU_C * GELU_A) * y2))
    half = 0.5 + 0.5 * t
    slope = half + (0.5 * y) * (1.0 - t * t) * (GELU_C + (3.0 * GELU_C * GELU_A) * y2)
    return y * half, slope


def retained(log_decay, carried):
    y = 2.0 * log_decay
    series = -y * (1.0 + y * (1 / 2 + y * (1 / 6 + y * (1 / 24 + y * (1 / 120)))))
    return jnp.maximum(jnp.where(y > -0.0625, series, 1.0 - carried * carried), 1e-36)


def at(j):
    return pl.ds(8 * j, 8)


def tile_params():
    return pltpu.CompilerParams(dimension_semantics=("arbitrary",), vmem_limit_bytes=VMEM_LIMIT)


def wide_block(width, tiles=None, column=0):
    row = (lambda t: t) if tiles is None else (lambda t: tiles - 1 - t)
    return pl.BlockSpec((ROWS, width), lambda t: (row(t), column))


def whole(a):
    return pl.BlockSpec(a.shape, lambda t: (0,) * a.ndim)


def fixed(*dims):
    return pl.BlockSpec(dims, lambda t: (0,) * len(dims))


def forward_kernel(
    bx_ref, prev_ref, mask_ref, par_ref, gates_ref,
    conv_ref, low_ref, r_ref, i_ref, state_ref, decay_ref,
    lags, pre, carry,
):
    width = bx_ref.shape[1]

    @pl.when(pl.program_id(0) == 0)
    def _():
        lags[...] = prev_ref[...]
        carry[at(0), :] = jnp.zeros((8, width), F32)
        carry[at(1), :] = jnp.ones((8, width), F32)

    past = [lags[at(2 - k), :] for k in range(3)]
    for j in range(STEPS):
        now = bx_ref[at(j), :]
        m = mask_ref[at(j), :]
        out = par_ref[pl.ds(0, 1), :] + par_ref[pl.ds(1, 1), :] * now
        for k in range(3):
            out = out + par_ref[pl.ds(2 + k, 1), :] * (past[k] * m[:, k + 1 : k + 2])
        conv_ref[at(j), :] = out
        past = [now, past[0], past[1]]
    for k in range(3):
        lags[at(2 - k), :] = past[k]
    low = conv_ref[...].astype(BF16)
    low_ref[...] = low
    pre[...] = jnp.dot(low, gates_ref[...], preferred_element_type=F32)

    state, decay = carry[at(0), :], carry[at(1), :]
    for j in range(STEPS):
        live = jnp.broadcast_to(mask_ref[at(j), :][:, 1:2], state.shape) != 0.0
        r = 1.0 / (1.0 + jnp.exp(-(pre[at(j), pl.ds(0, width)] + par_ref[pl.ds(5, 1), :])))
        i = 0.5 + 0.5 * jnp.tanh(
            0.5 * (pre[at(j), pl.ds(width, width)] + par_ref[pl.ds(6, 1), :])
        )
        log_decay = par_ref[pl.ds(7, 1), :] * r
        a = jnp.exp(log_decay)
        e = retained(log_decay, a)
        drive = jnp.where(live, e * lax.rsqrt(e), 1.0) * (i * conv_ref[at(j), :])
        a = jnp.where(live, a, 0.0)
        state = a * state + drive
        decay = a * decay
        r_ref[at(j), :] = r
        i_ref[at(j), :] = i
        state_ref[at(j), :] = state
        decay_ref[at(j), :] = decay
    carry[at(0), :] = state
    carry[at(1), :] = decay


def forward_recurrence(both, prev, masks, params, gates):
    tokens, width = both.shape[0], prev.shape[1]
    size = tokens * width
    wide = wide_block(width)
    shape = lambda d: jax.ShapeDtypeStruct((tokens, width), d)
    return pl.pallas_call(
        forward_kernel,
        name="forward_recurrence",
        grid=(tokens // ROWS,),
        in_specs=[
            wide, whole(prev), pl.BlockSpec((ROWS, 8), lambda t: (t, 0)), whole(params),
            whole(gates),
        ],
        out_specs=[wide] * 6,
        out_shape=[shape(F32), shape(BF16), shape(F32), shape(F32), shape(F32), shape(F32)],
        scratch_shapes=[
            pltpu.VMEM((24, width), F32),
            pltpu.VMEM((ROWS, 2 * width), F32),
            pltpu.VMEM((16, width), F32),
        ],
        compiler_params=tile_params(),
        cost_estimate=pl.CostEstimate(
            flops=4 * size * width, bytes_accessed=30 * size, transcendentals=6 * size
        ),
    )(both, prev, masks, params, gates)


def reverse_kernel(
    dm_ref, by_ref, r_ref, state_ref, mask_ref, par_ref,
    grad_ref, reach_ref, dby_ref, head_ref,
    slopes,
):
    width = dm_ref.shape[1]

    @pl.when(pl.program_id(0) == 0)
    def _():
        head_ref[at(0), :] = jnp.zeros((8, width), F32)
        head_ref[at(1), :] = jnp.ones((8, width), F32)

    u, reach = head_ref[at(0), :], head_ref[at(1), :]
    for j in range(STEPS - 1, -1, -1):
        d = dm_ref[at(j), :]
        act, slope = gelu_parts(by_ref[at(j), :])
        slopes[at(j), :] = slope * (state_ref[at(j), :] * d)
        live = jnp.broadcast_to(mask_ref[at(j), :][:, 1:2], u.shape) != 0.0
        a = jnp.where(live, jnp.exp(par_ref[pl.ds(7, 1), :] * r_ref[at(j), :]), 0.0)
        g = d * act + u
        grad_ref[at(j), :] = g
        reach_ref[at(j), :] = reach
        u = a * g
        reach = a * reach
    head_ref[at(0), :] = u
    head_ref[at(1), :] = reach
    dby_ref[...] = slopes[...].astype(BF16)


def reverse_recurrence(dm, both, r, state, masks, params):
    tokens, width = dm.shape
    tiles = tokens // ROWS
    wide = wide_block(width, tiles)
    shape = lambda d: jax.ShapeDtypeStruct(dm.shape, d)
    return pl.pallas_call(
        reverse_kernel,
        name="reverse_recurrence",
        grid=(tiles,),
        in_specs=[
            wide, wide_block(width, tiles, 1), wide, wide, wide_block(8, tiles), whole(params),
        ],
        out_specs=[wide, wide, wide, fixed(16, width)],
        out_shape=[shape(F32), shape(F32), shape(BF16), jax.ShapeDtypeStruct((16, width), F32)],
        scratch_shapes=[pltpu.VMEM((ROWS, width), F32)],
        compiler_params=tile_params(),
        cost_estimate=pl.CostEstimate(
            flops=30 * dm.size, bytes_accessed=26 * dm.size, transcendentals=2 * dm.size
        ),
    )(dm, both, r, state, masks, params)


def gate_grad_kernel(
    grad_ref, reach_ref, r_ref, i_ref, conv_ref, state_ref, before_ref, bx_ref, bx_before_ref,
    mask_ref, dby_ref, prev_ref, ends_ref, par_ref, gates_ref,
    out_ref, tail_ref, edge_ref, sums_ref, both_ref,
    pair, direct, ahead,
):
    width = grad_ref.shape[1]
    step_at = pl.program_id(0)
    first = step_at == pl.num_programs(0) - 1

    @pl.when(step_at == 0)
    def _():
        sums_ref[...] = jnp.zeros_like(sums_ref)
        edge_ref[...] = jnp.zeros_like(edge_ref)

    @pl.when(first)
    def _():
        ahead[at(0), :] = ends_ref[at(0), :]
        for k in range(3):
            ahead[at(1 + k), :] = prev_ref[at(2 - k), :]

    @pl.when(jnp.logical_not(first))
    def _():
        ahead[at(0), :] = before_ref[...]
        for k in range(3):
            ahead[at(1 + k), :] = bx_before_ref[at(3 - k), :]

    message = ends_ref[at(1), :]
    zero = jnp.zeros((8, width), F32)
    sum_r = sum_i = sum_d = zero
    slope = par_ref[pl.ds(7, 1), :]
    past = ahead[at(0), :]
    for j in range(STEPS):
        g = grad_ref[at(j), :] + reach_ref[at(j), :] * message
        r, i, conv = r_ref[at(j), :], i_ref[at(j), :], conv_ref[at(j), :]
        live = jnp.broadcast_to(mask_ref[at(j), :][:, 1:2], g.shape) != 0.0
        log_decay = slope * r
        a = jnp.exp(log_decay)
        e = retained(log_decay, a)
        inv = lax.rsqrt(e)
        s = jnp.where(live, e * inv, 1.0)
        gi = g * i
        gic = gi * conv
        d_log = jnp.where(live, a * (g * past - gic * (a * inv)), 0.0)
        d_r = d_log * r
        d_pa = (slope * d_r) * (1.0 - r)
        d_pi = (gic * s) * (1.0 - i)
        direct[at(j), :] = gi * s
        pair[at(j), pl.ds(0, width)] = d_pa
        pair[at(j), pl.ds(width, width)] = d_pi
        sum_r = sum_r + d_pa
        sum_i = sum_i + d_pi
        sum_d = sum_d + d_r
        past = state_ref[at(j), :]
    for n, total in enumerate((sum_r, sum_i, sum_d)):
        sums_ref[at(n), :] += total

    both = pair[...].astype(BF16)
    both_ref[...] = both
    direct[...] += contract_last(both, gates_ref[...])

    p1, p2, p3 = (edge_ref[at(k), :] for k in range(3))
    sums = [zero] * 5
    w = [par_ref[pl.ds(1 + k, 1), :] for k in range(4)]

    def behind(j, k):
        return bx_ref[at(j - k), :] if j >= k else ahead[at(k - j), :]

    for j in range(STEPS - 1, -1, -1):
        d = direct[at(j), :]
        m = mask_ref[at(j), :]
        d1, d2, d3 = (d * m[:, k : k + 1] for k in (1, 2, 3))
        direct[at(j), :] = w[0] * d + p1
        p1 = w[1] * d1 + p2
        p2 = w[2] * d2 + p3
        p3 = w[3] * d3
        for n, term in enumerate((d * behind(j, 0), d1 * behind(j, 1), d2 * behind(j, 2), d3 * behind(j, 3))):
            sums[n + 1] = sums[n + 1] + term
        sums[0] = sums[0] + d
    for n, total in enumerate(sums):
        sums_ref[at(3 + n), :] += total
    for k, p in enumerate((p1, p2, p3)):
        edge_ref[at(k), :] = p
    out_ref[:, pl.ds(0, width)] = direct[...].astype(BF16)
    out_ref[:, pl.ds(width, width)] = dby_ref[...]

    @pl.when(step_at == 0)
    def _():
        tail_ref[...] = direct[pl.ds(ROWS - 32, 32), :]


def gate_gradients(grad, reach, r, i, conv, state, both, masks, dby, prev, ends, params, gates):
    tokens, width = grad.shape
    tiles = tokens // ROWS
    wide = wide_block(width, tiles)
    ahead = lambda n: pl.BlockSpec(
        (n, width), lambda t: (jnp.maximum((tiles - 1 - t) * (ROWS // n) - 1, 0), 0)
    )
    return pl.pallas_call(
        gate_grad_kernel,
        name="gate_gradients",
        grid=(tiles,),
        in_specs=[
            wide, wide, wide, wide, wide, wide, ahead(8), wide, ahead(32), wide_block(8, tiles),
            wide, whole(prev), whole(ends), whole(params), whole(gates),
        ],
        out_specs=[
            wide_block(2 * width, tiles), fixed(32, width), fixed(24, width), fixed(64, width),
            wide_block(2 * width, tiles),
        ],
        out_shape=[
            jax.ShapeDtypeStruct((tokens, 2 * width), BF16),
            jax.ShapeDtypeStruct((32, width), F32),
            jax.ShapeDtypeStruct((24, width), F32),
            jax.ShapeDtypeStruct((64, width), F32),
            jax.ShapeDtypeStruct((tokens, 2 * width), BF16),
        ],
        scratch_shapes=[
            pltpu.VMEM((ROWS, 2 * width), F32),
            pltpu.VMEM((ROWS, width), F32),
            pltpu.VMEM((32, width), F32),
        ],
        compiler_params=tile_params(),
        cost_estimate=pl.CostEstimate(
            flops=4 * grad.size * width, bytes_accessed=38 * grad.size,
            transcendentals=2 * grad.size,
        ),
    )(grad, reach, r, i, conv, state, state, both, both, masks, dby, prev, ends, params, gates)


def settle_kernel(main_ref, tail_ref, edge_ref, beyond_ref, out_ref):
    del main_ref
    width = tail_ref.shape[1]
    row = lax.broadcasted_iota(jnp.int32, (8, width), 0)
    steps = [tail_ref[at(0), :]]
    for k in (2, 1, 0):
        up = pltpu.roll(edge_ref[at(k), :], 7, 0)
        up = jnp.where(row == 7, beyond_ref[pl.ds(k, 1), :], up)
        steps.append(tail_ref[at(3 - k), :] + up)
    out_ref[...] = jnp.concatenate(steps, axis=0).astype(BF16)


def settled(main, tail, edge, beyond):
    rows, width = tail.shape
    last = pl.BlockSpec((rows, width), lambda t: (main.shape[0] // rows - 1, 0))
    return pl.pallas_call(
        settle_kernel,
        name="settle",
        grid=(1,),
        in_specs=[last, whole(tail), whole(edge), whole(beyond)],
        out_specs=last,
        out_shape=jax.ShapeDtypeStruct(main.shape, main.dtype),
        input_output_aliases={0: 0},
        compiler_params=tile_params(),
        cost_estimate=pl.CostEstimate(flops=4 * tail.size, bytes_accessed=12 * tail.size, transcendentals=0),
    )(main, tail, edge, beyond)


def units_kernel(
    n2_ref, gate_ref, up_ref, d_hid_ref, hid_ref, d_gate_ref, d_up_ref, pull_ref
):
    tokens = n2_ref.shape[0]
    step_at = pl.program_id(0)
    rows = min(256, tokens)
    for t in range(tokens // rows):
        here = pl.ds(t * rows, rows)
        gate = dot(n2_ref[here, :], gate_ref[...])
        up = dot(n2_ref[here, :], up_ref[...])
        act, slope = gelu_parts(gate)
        d_hid = d_hid_ref[here, :]
        d_gate = (slope * up * d_hid).astype(BF16)
        d_up = (act * d_hid).astype(BF16)
        hid_ref[here, :] = (act * up).astype(BF16)
        d_gate_ref[here, :] = d_gate
        d_up_ref[here, :] = d_up
        pull = d_gate.astype(F32) * gate + d_up.astype(F32) * up
        pull = sum(pull[:, n : n + 128] for n in range(0, pull.shape[1], 128))

        @pl.when(step_at == 0)
        def _():
            pull_ref[here, :] = pull

        @pl.when(step_at > 0)
        def _():
            pull_ref[here, :] += pull


def mlp_units(n2, gate_weight, up_weight, d_hid):
    tokens, width = n2.shape
    units = d_hid.shape[1]
    each = 512 if units % 512 == 0 else 256
    column = lambda rows: pl.BlockSpec((rows, each), lambda j: (0, j))
    low = jax.ShapeDtypeStruct((tokens, units), BF16)
    return pl.pallas_call(
        units_kernel,
        name="mlp_units",
        grid=(units // each,),
        in_specs=[
            pl.BlockSpec((tokens, width), lambda j: (0, 0), pipeline_mode=pl.Buffered(1)),
            column(width), column(width), column(tokens),
        ],
        out_specs=[column(tokens)] * 3 + [pl.BlockSpec((tokens, 128), lambda j: (0, 0))],
        out_shape=[low, low, low, jax.ShapeDtypeStruct((tokens, 128), F32)],
        compiler_params=pltpu.CompilerParams(
            dimension_semantics=("arbitrary",), vmem_limit_bytes=48 << 20
        ),
        cost_estimate=pl.CostEstimate(
            flops=4 * tokens * width * units, transcendentals=tokens * units,
            bytes_accessed=2 * (tokens * width + 2 * width * units) + 10 * tokens * units,
        ),
    )(n2, gate_weight, up_weight, d_hid)


def shifted(x, axis, by):
    peers = lax.axis_size(axis)
    pairs = [(i, i + by) for i in range(peers) if 0 <= i + by < peers]
    return lax.ppermute(x, axis, pairs)


def bit_orders():
    bits = (lax.axis_size("seq") - 1).bit_length()
    outer = list(range(1, bits))
    return outer, outer[::-1]


def across(x, bit, axis="seq"):
    n = lax.axis_size(axis)
    return lax.ppermute(x, axis, [(i, i ^ (1 << bit)) for i in range(n)])


def own_bit(bit, axis="seq"):
    return (lax.axis_index(axis) >> bit) & 1


def relative(x, order, axis=1):
    n = lax.axis_size("seq")
    each = x.shape[axis] // n
    bits = len(order)
    out = []
    for place in range(n):
        number = sum(1 << bit for k, bit in enumerate(order) if place >> (bits - 1 - k) & 1)
        start = (lax.axis_index("seq") ^ number) * each
        out.append(lax.dynamic_slice_in_dim(x, start, each, axis))
    return jnp.concatenate(out, axis=axis)


def crossed(x, bit, axis):
    half = x.shape[axis] // 2
    give = lax.slice_in_dim(x, half, 2 * half, axis=axis).astype(BF16)
    keep = lax.slice_in_dim(x, 0, half, axis=axis).astype(F32)
    return keep + across(give, bit).astype(F32)


def exchanged(x, axis):
    n = lax.axis_size(axis)
    for bit in range((n - 1).bit_length()):
        x = x + across(x, bit, axis)
    return x


def places(order):
    n = lax.axis_size("seq")
    away = lax.axis_index("seq") ^ jnp.arange(n, dtype=jnp.int32)
    bits = len(order)
    return sum(((away >> bit) & 1) << (bits - 1 - k) for k, bit in enumerate(order))


def picked(own_a, far_a, own_b, far_b, tables, fill, outs, name):
    n = lax.axis_size("seq")
    half = n // 2

    def kernel(at_a, at_b, own_a_ref, far_a_ref, own_b_ref, far_b_ref, *refs):
        step_at = pl.program_id(0)
        for at, side, own, far in ((at_a, 0, own_a_ref, far_a_ref), (at_b, 1, own_b_ref, far_b_ref)):
            near = at[step_at] < half

            @pl.when(near)
            def _():
                fill(side, own, refs)

            @pl.when(jnp.logical_not(near))
            def _():
                fill(side, far, refs)

    def pick(array, which, far):
        def block(s, *at):
            here, other = at[which][s], at[which][s ^ 1]
            return array[2](lax.rem(jnp.where((here >= half) == far, here, other), half))

        return pl.BlockSpec(array[1], block)

    arrays = (own_a, far_a, own_b, far_b)
    return pl.pallas_call(
        kernel,
        name=name,
        grid_spec=pltpu.PrefetchScalarGridSpec(
            num_scalar_prefetch=2,
            grid=(n,),
            in_specs=[
                pick(own_a, 0, False), pick(far_a, 0, True), pick(own_b, 1, False),
                pick(far_b, 1, True),
            ],
            out_specs=[pl.BlockSpec(block, at) for _, block, at in outs],
        ),
        out_shape=[shape for shape, _, _ in outs],
        compiler_params=pltpu.CompilerParams(
            dimension_semantics=("arbitrary",), vmem_limit_bytes=40 << 20
        ),
        cost_estimate=pl.CostEstimate(
            flops=0, transcendentals=0,
            bytes_accessed=sum(a[0].size * 2 for a in arrays) + sum(o[0].size * 4 for o in outs),
        ),
    )(*tables, *(a[0] for a in arrays))


def ordered(own_a, far_a, own_b, far_b, tables, outputs, name):
    n = lax.axis_size("seq")
    each = own_a.shape[1] // (n // 2)
    wrap = lambda a: (a, (a.shape[0], each), lambda place: (0, place))

    def fill(side, ref, refs):
        for out, pieces in zip(refs, outputs):
            row = 0
            for route, start, rows in pieces:
                if route == side:
                    out[pl.ds(row, rows), :] = ref[pl.ds(start, rows), :].astype(F32)
                row += rows

    heights = [sum(rows for _, _, rows in pieces) for pieces in outputs]
    outs = [
        (jax.ShapeDtypeStruct((h, n * each), F32), (h, each), lambda s, *at: (0, s))
        for h in heights
    ]
    return picked(wrap(own_a), wrap(far_a), wrap(own_b), wrap(far_b), tables, fill, outs, name)


def joined(x, order):
    x = x[None]
    for bit in order:
        x = jnp.concatenate([x, across(x, bit)])
    return x


def mlp_weights(own_a, far_a, own_b, far_b, tables, lead):
    n = lax.axis_size("seq")
    units = own_a.shape[2]
    cut = own_a.shape[1] - lead
    wrap = lambda a: (a, (1, *a.shape[1:]), lambda place: (place, 0, 0))

    def fill(side, ref, refs):
        refs[side][0] = ref[0, pl.ds(0, lead), :]
        refs[2][0, side] = ref[0, pl.ds(lead, cut), :]

    full = (jax.ShapeDtypeStruct((n, lead, units), BF16), (1, lead, units), lambda s, *at: (s, 0, 0))
    down = (
        jax.ShapeDtypeStruct((n, 2, cut, units), BF16), (1, 2, cut, units),
        lambda s, *at: (s, 0, 0, 0),
    )
    gate, up, down = picked(
        wrap(own_a), wrap(far_a), wrap(own_b), wrap(far_b), tables, fill, [full, full, down], "mlp_weights"
    )
    return gate.reshape(-1, units), up.reshape(-1, units), down.reshape(-1, units)


def output_rows(own_a, far_a, own_b, far_b, tables):
    n = lax.axis_size("seq")
    _, groups, part, middle = own_a.shape
    wrap = lambda a: (a, (1, *a.shape[1:]), lambda place: (place, 0, 0, 0))

    def fill(side, ref, refs):
        refs[0][:, 0, :, pl.ds(side * middle, middle)] = ref[0]

    out = (
        jax.ShapeDtypeStruct((groups, n, part, 2 * middle), BF16), (groups, 1, part, 2 * middle),
        lambda s, *at: (0, s, 0, 0),
    )
    return picked(
        wrap(own_a), wrap(far_a), wrap(own_b), wrap(far_b), tables, fill, [out], "output_rows"
    )[0].reshape(-1, 2 * middle)


def chained(decays, values, place, reverse):
    devices, stretches = decays.shape[:2]
    total = jnp.zeros_like(values[0, 0])
    out = []
    hops = [(d, s) for d in range(devices) for s in range(stretches)]
    own_d = lax.dynamic_index_in_dim(decays, place, 0, False)
    own_v = lax.dynamic_index_in_dim(values, place, 0, False)
    order = range(stretches - 1, -1, -1) if reverse else range(stretches)
    whole_d, whole_v = [], []
    for d in range(devices):
        decay, value = jnp.ones_like(total), jnp.zeros_like(total)
        for s in order:
            value = values[d, s] + decays[d, s] * value
            decay = decay * decays[d, s]
        whole_d.append(decay)
        whole_v.append(value)
    for hop in range(devices - 1):
        d = devices - 1 - hop if reverse else hop
        live = d > place if reverse else d < place
        total = jnp.where(live, whole_v[d] + whole_d[d] * total, total)
    for s in order:
        out.append(total)
        total = own_v[s] + own_d[s] * total
    return jnp.stack(out[::-1] if reverse else out)


def gelu(y):
    return y * (0.5 + 0.5 * jnp.tanh(y * (GELU_C + (GELU_C * GELU_A) * (y * y))))


def side_by_side(x):
    rows = x.shape[0]
    return jnp.swapaxes(x.reshape(8, rows // 8, *x.shape[1:]), 0, 1).reshape(x.shape)


def in_order(x):
    rows = x.shape[0]
    return jnp.swapaxes(x.reshape(rows // 8, 8, *x.shape[1:]), 0, 1).reshape(x.shape)


def block_diagonal(blocks, padded):
    count, size, _ = blocks.shape
    rows = [
        jnp.pad(blocks[b], ((0, 0), (b * size, padded - (b + 1) * size))) for b in range(count)
    ]
    return jnp.pad(jnp.concatenate(rows, axis=0), ((0, padded - count * size), (0, 0)))


def after(value, *others):
    return lax.optimization_barrier((value, *others))[0]


def row_major(x):
    return with_layout_constraint(x, Layout(major_to_minor=tuple(range(x.ndim))))


def gather_features(x):
    return lax.all_gather(x, "tp", axis=1, tiled=True)


def scatter_features(x):
    return lax.psum_scatter(x.astype(BF16), "tp", scatter_dimension=1, tiled=True).astype(F32)


def on_device(
    hidden_in, segment_ids, first_gain, input_weight, gelu_weight, conv_weight, conv_bias,
    recur_gate, input_gate, recur_bias, input_bias, decay_param, output_weight, second_gain,
    gate_weight, up_weight, down_weight, grad_out,
):
    tokens, share = hidden_in.shape
    channels = input_weight.shape[1]
    padded = -(-channels // 128) * 128
    extra = padded - channels
    taps = conv_weight.shape[0]
    halo = taps - 1
    blocks, size = recur_gate.shape[0], recur_gate.shape[1]
    width = grad_out.shape[1]
    units = gate_weight.shape[1]
    seq_devices = lax.axis_size("seq")
    tp_devices = lax.axis_size("tp")
    seq_place = lax.axis_index("seq")
    share_start = lax.axis_index("tp") * share
    order_a, order_b = bit_orders()

    route_a, route_b = [0, *order_a], [0, *order_b]

    x_low = side_by_side(hidden_in)
    full = gather_features(x_low)

    down_t = down_weight.T
    lead = down_t.shape[0]
    cut = lead // 2
    legs = [
        (jnp.concatenate([gate_weight, down_t[:cut]]), order_a),
        (jnp.concatenate([up_weight, down_t[cut:]]), order_b),
    ]
    first = [joined(a, order[:-1]) for a, order in legs]
    (
        segment_ids, input_weight, gelu_weight, recur_gate, input_gate, output_weight, grad_out,
        *first,
    ) = lax.optimization_barrier(
        (segment_ids, input_weight, gelu_weight, recur_gate, input_gate, output_weight, grad_out, *first)
    )
    second = [across(a, order[-1]) for a, (_, order) in zip(first, legs)]
    part = channels // seq_devices
    own_rows = lax.dynamic_slice_in_dim(output_weight, seq_place * part, part, 0)

    ids = segment_ids.astype(F32)
    prev_ids = shifted(ids[tokens - halo :], "seq", 1)
    prev_ids = jnp.where(seq_place == 0, -1.0, prev_ids)
    next_id = jnp.where(seq_place == seq_devices - 1, -1.0, shifted(ids[:1], "seq", -1))
    ext = jnp.concatenate([prev_ids, ids])
    same = [(ext[halo - k : halo - k + tokens] == ids).astype(F32) for k in range(taps)]
    masks = side_by_side(jnp.stack(same + [jnp.zeros_like(ids)] * (8 - taps), axis=1))
    next_ids = jnp.concatenate([ids[1:], next_id])
    closing = (next_ids != ids).astype(F32)[None, :]
    member = (segment_ids[None, :] == jnp.arange(SEGS, dtype=jnp.int32)[:, None]).astype(F32)
    picks = side_by_side((member * closing).T).T

    slope = -DECAY_SCALE * jax.nn.softplus(-decay_param)
    params = jnp.concatenate(
        [jnp.stack([conv_bias]), conv_weight, jnp.stack([recur_bias, input_bias, slope])], axis=0
    )
    params = jnp.pad(params, ((0, 0), (0, extra)))
    gates = jnp.concatenate(
        [block_diagonal(recur_gate, padded), block_diagonal(input_gate, padded)], axis=1
    )
    pad_rows = lambda a: jnp.pad(a, ((0, extra), (0, 0)))
    branch_weight = jnp.concatenate([pad_rows(input_weight.T), pad_rows(gelu_weight.T)], axis=0)
    output_padded = pad_rows(output_weight)
    grad_rows = side_by_side(grad_out)
    params, gates, branch_weight, output_padded, grad_rows, masks, own_rows, full = (
        lax.optimization_barrier(
            (params, gates, branch_weight, output_padded, grad_rows, masks, own_rows, full)
        )
    )

    x = full.astype(F32)
    r1 = lax.rsqrt(jnp.mean(x * x, axis=1, keepdims=True) + EPSILON)
    n1 = (x * r1 * first_gain).astype(BF16)
    both = row_major(contract_last(n1, branch_weight))
    last = both[tokens - 8 * halo :, :padded].reshape(halo, 8, padded)
    before = shifted(last[:, 7], "seq", 1)
    prev = jnp.concatenate([before[:, None], last[:, :7]], axis=1).reshape(8 * halo, padded)
    over_tp = lax.all_gather(own_rows, "tp", axis=0, tiled=True)
    both, *second = lax.optimization_barrier((both, *second))
    conv, low, r, i, local, reach = forward_recurrence(both, prev, masks, params, gates)
    ends = jnp.stack([reach[tokens - 8 :], local[tokens - 8 :]])
    ends, over_tp = lax.optimization_barrier((ends, over_tp))
    ends = lax.all_gather(ends, "seq", axis=0)
    incoming = chained(ends[:, 0], ends[:, 1], seq_place, False)
    steps = lambda a: a.reshape(tokens // 8, 8, padded)
    state = (steps(local) + steps(reach) * incoming[None]).reshape(tokens, padded)
    mixed = (gelu(both[:, padded : padded + channels]) * state[:, :channels]).astype(BF16)
    mixed_full = lax.all_gather(mixed, "tp", axis=1, tiled=True)
    over_tp, _ = lax.optimization_barrier((over_tp, mixed))
    over_tp = over_tp.reshape(tp_devices, part, width)
    middle = width // 2
    rows_a = joined(over_tp[:, :, :middle], order_a)
    rows_b = joined(over_tp[:, :, middle:], order_b)
    grad_rows, *held = lax.optimization_barrier((grad_rows, *first, *second, mixed))
    own_a, own_b = (
        jnp.concatenate([held[leg], held[leg + len(legs)]]) for leg in range(len(legs))
    )
    tables = places([0, *order_a[::-1]]), places([0, *order_b[::-1]])
    gate_full, up_full, down_full = mlp_weights(
        own_a, across(own_a, 0), own_b, across(own_b, 0), tables, lead
    )
    d_hid = dot(grad_rows, down_full)
    output_full = output_rows(rows_a, across(rows_a, 0), rows_b, across(rows_b, 0), tables)
    d_hid, output_full, gate_full, up_full = lax.optimization_barrier(
        (d_hid, output_full, gate_full, up_full)
    )
    resid = x + dot(mixed_full, output_full)

    r2 = lax.rsqrt(jnp.mean(resid * resid, axis=1, keepdims=True) + EPSILON)
    n2 = (resid * r2 * second_gain).astype(BF16)
    hid, d_gate, d_up, pull2 = mlp_units(n2, gate_full, up_full, d_hid)
    d_n2_part = (contract_last(d_gate, gate_full) + contract_last(d_up, up_full)).astype(BF16)
    d_n2 = scatter_features(d_n2_part)
    n2_w, hid_w, pull2 = lax.optimization_barrier((n2, hid, pull2, d_n2_part))[:3]
    pull2 = lax.psum(jnp.sum(pull2, axis=1), "tp")[:, None]
    grad_w = after(grad_rows, d_n2_part)
    grad_a, grad_b = relative(grad_w, route_a), relative(grad_w, route_b)
    half = units // 2
    n2_a, n2_b = relative(n2_w, route_a), relative(n2_w, route_b)
    products = [
        (n2_a, d_gate, order_a), (n2_b, d_up, order_b),
        (grad_a, hid_w[:, :half], order_a), (grad_b, hid_w[:, half:], order_b),
    ]
    middle = width // 2
    gives = [across(contract_first(l[:, middle:], r).astype(BF16), 0) for l, r, _ in products]
    sums2 = [
        contract_first(l[:, :middle], r) + give.astype(F32)
        for (l, r, _), give in zip(products, gives)
    ]
    d_n2, pull2, *sums2 = lax.optimization_barrier((d_n2, pull2, *sums2))
    gain_share = lax.dynamic_slice_in_dim(second_gain, share_start, share)
    scaled = d_n2 * gain_share * r2
    scaled_low = scaled.astype(BF16)
    scaled_full = gather_features(scaled_low)
    hid_w, state_w, resid_w, d_n2_w, n1_w, _, *sums2 = lax.optimization_barrier(
        (hid_w, state, resid, d_n2, n1, scaled_low, *sums2)
    )
    n1_a, n1_b = relative(n1_w, route_a), relative(n1_w, route_b)
    finals = jnp.dot(picks, state_w, precision=lax.Precision.HIGHEST, preferred_element_type=F32)
    resid_share = lax.dynamic_slice_in_dim(resid_w, share_start, share, 1)
    grad_second = jnp.sum(d_n2_w * resid_share * r2, axis=0)
    mlp = contract_last(hid_w, down_full).astype(BF16)
    for leg in range(len(order_a) - 1):
        sums2 = [crossed(v, order[leg], 0) for v, (_, _, order) in zip(sums2, products)]
    centre = r2 * r2 * pull2 * (1.0 / width)
    last_gives = [v[v.shape[0] // 2 :].astype(BF16) for v in sums2]
    kept2 = [v[: v.shape[0] // 2] for v in sums2]
    scaled_full, mlp, finals, grad_second, n1_a, n1_b, *last_gives = lax.optimization_barrier(
        (scaled_full, mlp, finals, grad_second, n1_a, n1_b, *last_gives)
    )
    mlp_sum = lax.psum_scatter(mlp, "tp", scatter_dimension=1, tiled=True)
    d_resid_low = (
        grad_rows.astype(F32) + scaled_full.astype(F32) - resid * centre
    ).astype(BF16)
    last_gives = [across(v, order[-1]) for v, (_, _, order) in zip(last_gives, products)]

    dm = row_major(contract_last(d_resid_low, output_padded))
    grad_local, reach_back, dby, heads = reverse_recurrence(dm, both, r, state, masks, params)
    heads, *last_gives = lax.optimization_barrier((heads, *last_gives))
    outgoing = lax.all_gather(heads.reshape(2, 8, padded), "seq", axis=0)
    message = chained(outgoing[:, 1], outgoing[:, 0], seq_place, True)
    border = jnp.concatenate([incoming, message])
    d_main, tail, edge, sums, pair = gate_gradients(
        grad_local, reach_back, r, i, conv, state, both, masks, dby, prev, border, params, gates
    )
    beyond = shifted(edge.reshape(halo, 8, padded)[:, 0], "seq", -1)
    d_branch = settled(d_main, tail, edge, beyond)
    d_n1_part = dot(d_branch, branch_weight).astype(BF16)
    d_n1_part, mlp_sum = lax.optimization_barrier((d_n1_part, mlp_sum))
    d_n1 = scatter_features(d_n1_part)
    d_branch_w, pair, sums, d_n1_w = lax.optimization_barrier((d_branch, pair, sums, d_n1_part))
    dbx_w, dby_w = d_branch_w[:, :channels], d_branch_w[:, padded : padded + channels]
    back = lambda l, r: contract_first(l, r[:, middle:]).astype(BF16)
    front = lambda l, r: contract_first(l, r[:, :middle])
    give_a, give_b = back(dbx_w, n1_a), back(dby_w, n1_b)
    give_a, give_b, pair, sums, d_resid_w, d_n1_w, dbx_w, dby_w = lax.optimization_barrier(
        (give_a, give_b, pair, sums, d_resid_low, d_n1_w, dbx_w, dby_w)
    )

    def rest(total_a, total_b):
        for bit_a, bit_b in zip(order_a, order_b):
            total_a, total_b = crossed(total_a, bit_a, 1), crossed(total_b, bit_b, 1)
        total_a, total_b = total_a.astype(BF16), total_b.astype(BF16)
        alone = total_a, total_b
        for bit_a, bit_b in zip(order_a[::-1], order_b[::-1]):
            total_a = jnp.concatenate([total_a, across(total_a, bit_a)], axis=1)
            total_b = jnp.concatenate([total_b, across(total_b, bit_b)], axis=1)
        return alone, (total_a, across(total_a, 0), total_b, across(total_b, 0))

    far_a, far_b = across(give_a, 0), across(give_b, 0)
    ready, branch_parts = rest(
        front(dbx_w, n1_a) + far_a.astype(F32), front(dby_w, n1_b) + far_b.astype(F32)
    )
    first_part = jnp.sum(d_n1_w.astype(F32) * n1.astype(F32), axis=0) / first_gain
    pull1 = jnp.sum(d_n1_w.astype(F32) * n1.astype(F32), axis=1)
    second_part = lax.dynamic_update_slice(jnp.zeros((width,), F32), grad_second, (share_start,))
    over_tp = exchanged(jnp.concatenate([pull1, first_part, second_part]), "tp")
    pull1, gains = over_tp[:tokens, None], over_tp[tokens:]
    resid_a, resid_b = relative(d_resid_w, route_a), relative(d_resid_w, route_b)
    cut = channels // 2
    mixed_a, mixed_b = mixed[:, :cut], mixed[:, cut:]
    gate_grads = contract_first(low, pair)
    corner = lambda n, b: gate_grads[
        b * size : (b + 1) * size, n * padded + b * size : n * padded + (b + 1) * size
    ]
    corners = jnp.concatenate([corner(n, b) for b in range(blocks) for n in (0, 1)], axis=1)
    corners = jnp.pad(corners, ((0, 0), (0, width - corners.shape[1])))
    corners = relative(corners, route_b)
    sums = jnp.sum(sums.reshape(8, 8, padded), axis=1)
    small = jnp.concatenate([sums, finals], axis=0)[:, :channels]
    packed = jnp.concatenate([gains, small.reshape(-1)])
    packed = jnp.pad(packed, (0, -packed.size % (8 * width))).reshape(-1, width)
    few = packed.shape[0]
    packed = relative(packed, route_a)
    far_a = across(
        jnp.concatenate([back(mixed_a, resid_a), packed[:, middle:].astype(BF16)]), 0
    )
    far_b = across(
        jnp.concatenate([back(mixed_b, resid_b), corners[:, middle:].astype(BF16)]), 0
    )
    _, other_parts = rest(
        jnp.concatenate(
            [
                front(mixed_a, resid_a) + far_a[:cut].astype(F32),
                packed[:, :middle] + far_a[cut:].astype(F32),
            ]
        ),
        jnp.concatenate(
            [
                front(mixed_b, resid_b) + far_b[:cut].astype(F32),
                corners[:, :middle] + far_b[cut:].astype(F32),
            ]
        ),
    )

    kept2, last_gives, mlp_sum, d_n1, resid_share = lax.optimization_barrier(
        (kept2, last_gives, mlp_sum, d_n1, resid_share, ready)
    )[:5]
    done2 = [v + give.astype(F32) for v, give in zip(kept2, last_gives)]
    grad_gate_weight, grad_up_weight = done2[:2]
    grad_down_weight = jnp.concatenate(done2[2:], axis=1).T
    g_share = lax.dynamic_slice_in_dim(grad_rows, share_start, share, 1).astype(F32)
    d_resid_share = g_share + scaled - resid_share * centre
    block_out = in_order((resid_share + mlp_sum.astype(F32)).astype(BF16))
    gain1_share = lax.dynamic_slice_in_dim(first_gain, share_start, share)
    grad_in = (
        d_resid_share
        + d_n1 * gain1_share * r1
        - x_low.astype(F32) * (r1 * r1 * pull1 * (1.0 / width))
    )
    grad_in = in_order(grad_in.astype(BF16))
    tables = places(route_a), places(route_b)
    grad_input, grad_gelu = ordered(
        *branch_parts, tables, [[(0, 0, channels)], [(1, 0, channels)]], "branch_gradients"
    )
    done = (block_out, grad_in, grad_gate_weight, grad_up_weight, grad_down_weight, grad_input, grad_gelu)
    other_parts, done = lax.optimization_barrier((other_parts, done))
    block_out, grad_in, grad_gate_weight, grad_up_weight, grad_down_weight, grad_input, grad_gelu = done
    grad_output_weight, packed, corners = ordered(
        *other_parts,
        tables,
        [[(0, 0, cut), (1, 0, cut)], [(0, cut, few)], [(1, cut, size)]],
        "other_gradients",
    )
    packed = packed.reshape(-1)
    gains = packed[: 2 * width]
    small = packed[2 * width : 2 * width + small.size].reshape(small.shape)
    corners = jnp.swapaxes(corners[:, : 2 * blocks * size].reshape(size, blocks, 2, size), 0, 1)
    grad_decay = small[2] * (DECAY_SCALE * jax.nn.sigmoid(-decay_param))
    return (
        block_out,
        grad_in,
        gains[:width],
        grad_input.T,
        grad_gelu.T,
        small[4:8],
        small[3],
        corners[:, :, 0],
        corners[:, :, 1],
        small[0],
        small[1],
        grad_decay,
        grad_output_weight,
        gains[width:],
        grad_gate_weight,
        grad_up_weight,
        grad_down_weight,
        small[8:],
    )


def solution(mesh):
    row = P("tp")
    return jax.shard_map(
        on_device,
        mesh=mesh,
        in_specs=(
            P("seq", "tp"), P("seq"), P(), P(None, "tp"), P(None, "tp"), P(None, "tp"), row,
            P("tp", None, None), P("tp", None, None), row, row, row, P("tp", None), P(),
            P("seq", "tp"), P("seq", "tp"), P("tp", "seq"), P("seq", None),
        ),
        out_specs=(
            P("seq", "tp"), P("seq", "tp"), P(), P(None, "tp"), P(None, "tp"), P(None, "tp"), row,
            P("tp", None, None), P("tp", None, None), row, row, row, P("tp", None), P(),
            P("seq", "tp"), P("seq", "tp"), P("tp", "seq"), P(None, "tp"),
        ),
        check_vma=False,
    )
```

```python
import jax
import jax.numpy as jnp
from jax import lax
from jax.experimental import pallas as pl
from jax.experimental.layout import Layout, with_layout_constraint
from jax.experimental.pallas import tpu as pltpu
from jax.sharding import PartitionSpec as P

SEGS = 8
EPSILON = 1e-06
DECAY_SCALE = 8.0
GELU_C = 0.7978845608028654
GELU_A = 0.044715
F32 = jnp.float32
BF16 = jnp.bfloat16
VMEM_LIMIT = 58 << 20
STEPS = 16
ROWS = 8 * STEPS


def dot(left, right):
    return jnp.dot(left, right, preferred_element_type=F32)


def contract_first(left, right):
    return lax.dot_general(left, right, (((0,), (0,)), ((), ())), preferred_element_type=F32)


def contract_last(left, right):
    return lax.dot_general(left, right, (((1,), (1,)), ((), ())), preferred_element_type=F32)


def gelu_parts(y):
    y2 = y * y
    t = jnp.tanh(y * (GELU_C + (GELU_C * GELU_A) * y2))
    half = 0.5 + 0.5 * t
    slope = half + (0.5 * y) * (1.0 - t * t) * (GELU_C + (3.0 * GELU_C * GELU_A) * y2)
    return y * half, slope


def retained(log_decay, carried):
    y = 2.0 * log_decay
    series = -y * (1.0 + y * (1 / 2 + y * (1 / 6 + y * (1 / 24 + y * (1 / 120)))))
    return jnp.maximum(jnp.where(y > -0.0625, series, 1.0 - carried * carried), 1e-36)


def at(j):
    return pl.ds(8 * j, 8)


def tile_params():
    return pltpu.CompilerParams(dimension_semantics=("arbitrary",), vmem_limit_bytes=VMEM_LIMIT)


def wide_block(width, tiles=None, column=0):
    row = (lambda t: t) if tiles is None else (lambda t: tiles - 1 - t)
    return pl.BlockSpec((ROWS, width), lambda t: (row(t), column))


def whole(a):
    return pl.BlockSpec(a.shape, lambda t: (0,) * a.ndim)


def fixed(*dims):
    return pl.BlockSpec(dims, lambda t: (0,) * len(dims))


def forward_kernel(
    bx_ref, prev_ref, mask_ref, par_ref, gates_ref,
    conv_ref, low_ref, r_ref, i_ref, state_ref, decay_ref,
    lags, pre, carry,
):
    width = bx_ref.shape[1]

    @pl.when(pl.program_id(0) == 0)
    def _():
        lags[...] = prev_ref[...]
        carry[at(0), :] = jnp.zeros((8, width), F32)
        carry[at(1), :] = jnp.ones((8, width), F32)

    past = [lags[at(2 - k), :] for k in range(3)]
    for j in range(STEPS):
        now = bx_ref[at(j), :]
        m = mask_ref[at(j), :]
        out = par_ref[pl.ds(0, 1), :] + par_ref[pl.ds(1, 1), :] * now
        for k in range(3):
            out = out + par_ref[pl.ds(2 + k, 1), :] * (past[k] * m[:, k + 1 : k + 2])
        conv_ref[at(j), :] = out
        past = [now, past[0], past[1]]
    for k in range(3):
        lags[at(2 - k), :] = past[k]
    low = conv_ref[...].astype(BF16)
    low_ref[...] = low
    pre[...] = jnp.dot(low, gates_ref[...], preferred_element_type=F32)

    state, decay = carry[at(0), :], carry[at(1), :]
    for j in range(STEPS):
        live = jnp.broadcast_to(mask_ref[at(j), :][:, 1:2], state.shape) != 0.0
        r = 1.0 / (1.0 + jnp.exp(-(pre[at(j), pl.ds(0, width)] + par_ref[pl.ds(5, 1), :])))
        i = 0.5 + 0.5 * jnp.tanh(
            0.5 * (pre[at(j), pl.ds(width, width)] + par_ref[pl.ds(6, 1), :])
        )
        log_decay = par_ref[pl.ds(7, 1), :] * r
        a = jnp.exp(log_decay)
        e = retained(log_decay, a)
        drive = jnp.where(live, e * lax.rsqrt(e), 1.0) * (i * conv_ref[at(j), :])
        a = jnp.where(live, a, 0.0)
        state = a * state + drive
        decay = a * decay
        r_ref[at(j), :] = r
        i_ref[at(j), :] = i
        state_ref[at(j), :] = state
        decay_ref[at(j), :] = decay
    carry[at(0), :] = state
    carry[at(1), :] = decay


def forward_recurrence(both, prev, masks, params, gates):
    tokens, width = both.shape[0], prev.shape[1]
    size = tokens * width
    wide = wide_block(width)
    shape = lambda d: jax.ShapeDtypeStruct((tokens, width), d)
    return pl.pallas_call(
        forward_kernel,
        name="forward_recurrence",
        grid=(tokens // ROWS,),
        in_specs=[
            wide, whole(prev), pl.BlockSpec((ROWS, 8), lambda t: (t, 0)), whole(params),
            whole(gates),
        ],
        out_specs=[wide] * 6,
        out_shape=[shape(F32), shape(BF16), shape(F32), shape(F32), shape(F32), shape(F32)],
        scratch_shapes=[
            pltpu.VMEM((24, width), F32),
            pltpu.VMEM((ROWS, 2 * width), F32),
            pltpu.VMEM((16, width), F32),
        ],
        compiler_params=tile_params(),
        cost_estimate=pl.CostEstimate(
            flops=4 * size * width, bytes_accessed=30 * size, transcendentals=6 * size
        ),
    )(both, prev, masks, params, gates)


def reverse_kernel(
    grad_in_ref, scaled_ref, n2_ref, factor_ref, gain_ref, weight_ref, by_ref, r_ref, state_ref,
    mask_ref, par_ref,
    resid_ref, grad_ref, reach_ref, dby_ref, head_ref,
    dm, slopes,
):
    width = by_ref.shape[1]

    @pl.when(pl.program_id(0) == 0)
    def _():
        head_ref[at(0), :] = jnp.zeros((8, width), F32)
        head_ref[at(1), :] = jnp.ones((8, width), F32)

    centred = (n2_ref[...].astype(F32) * gain_ref[...]) * factor_ref[...]
    d_resid = grad_in_ref[...].astype(F32) + scaled_ref[...].astype(F32) - centred
    d_resid = d_resid.astype(BF16)
    resid_ref[...] = d_resid
    dm[...] = contract_last(d_resid, weight_ref[...])

    u, reach = head_ref[at(0), :], head_ref[at(1), :]
    for j in range(STEPS - 1, -1, -1):
        d = dm[at(j), :]
        act, slope = gelu_parts(by_ref[at(j), :])
        slopes[at(j), :] = slope * (state_ref[at(j), :] * d)
        live = jnp.broadcast_to(mask_ref[at(j), :][:, 1:2], u.shape) != 0.0
        a = jnp.where(live, jnp.exp(par_ref[pl.ds(7, 1), :] * r_ref[at(j), :]), 0.0)
        g = d * act + u
        grad_ref[at(j), :] = g
        reach_ref[at(j), :] = reach
        u = a * g
        reach = a * reach
    head_ref[at(0), :] = u
    head_ref[at(1), :] = reach
    dby_ref[...] = slopes[...].astype(BF16)


def reverse_recurrence(grad_rows, scaled, n2, factor, gain, weight, both, r, state, masks, params):
    tokens, full = grad_rows.shape
    width = weight.shape[0]
    tiles = tokens // ROWS
    wide = wide_block(width, tiles)
    whole_row = wide_block(full, tiles)
    shape = lambda n, d: jax.ShapeDtypeStruct((tokens, n), d)
    return pl.pallas_call(
        reverse_kernel,
        name="reverse_recurrence",
        grid=(tiles,),
        in_specs=[
            whole_row, whole_row, whole_row, wide_block(1, tiles), whole(gain), whole(weight),
            wide_block(width, tiles, 1), wide, wide, wide_block(8, tiles), whole(params),
        ],
        out_specs=[whole_row, wide, wide, wide, fixed(16, width)],
        out_shape=[
            shape(full, BF16), shape(width, F32), shape(width, F32), shape(width, BF16),
            jax.ShapeDtypeStruct((16, width), F32),
        ],
        scratch_shapes=[pltpu.VMEM((ROWS, width), F32), pltpu.VMEM((ROWS, width), F32)],
        compiler_params=tile_params(),
        cost_estimate=pl.CostEstimate(
            flops=2 * tokens * width * full, bytes_accessed=tokens * (8 * full + 24 * width),
            transcendentals=2 * tokens * width,
        ),
    )(grad_rows, scaled, n2, factor, gain, weight, both, r, state, masks, params)


def gate_grad_kernel(
    grad_ref, reach_ref, r_ref, i_ref, conv_ref, state_ref, before_ref, bx_ref, bx_before_ref,
    mask_ref, prev_ref, ends_ref, par_ref, gates_ref,
    out_ref, tail_ref, edge_ref, sums_ref, both_ref,
    pair, direct, ahead,
):
    width = grad_ref.shape[1]
    step_at = pl.program_id(0)
    first = step_at == pl.num_programs(0) - 1

    @pl.when(step_at == 0)
    def _():
        sums_ref[...] = jnp.zeros_like(sums_ref)
        edge_ref[...] = jnp.zeros_like(edge_ref)

    @pl.when(first)
    def _():
        ahead[at(0), :] = ends_ref[at(0), :]
        for k in range(3):
            ahead[at(1 + k), :] = prev_ref[at(2 - k), :]

    @pl.when(jnp.logical_not(first))
    def _():
        ahead[at(0), :] = before_ref[...]
        for k in range(3):
            ahead[at(1 + k), :] = bx_before_ref[at(3 - k), :]

    message = ends_ref[at(1), :]
    zero = jnp.zeros((8, width), F32)
    sum_r = sum_i = sum_d = zero
    slope = par_ref[pl.ds(7, 1), :]
    past = ahead[at(0), :]
    for j in range(STEPS):
        g = grad_ref[at(j), :] + reach_ref[at(j), :] * message
        r, i, conv = r_ref[at(j), :], i_ref[at(j), :], conv_ref[at(j), :]
        live = jnp.broadcast_to(mask_ref[at(j), :][:, 1:2], g.shape) != 0.0
        log_decay = slope * r
        a = jnp.exp(log_decay)
        e = retained(log_decay, a)
        inv = lax.rsqrt(e)
        s = jnp.where(live, e * inv, 1.0)
        gi = g * i
        gic = gi * conv
        d_log = jnp.where(live, a * (g * past - gic * (a * inv)), 0.0)
        d_r = d_log * r
        d_pa = (slope * d_r) * (1.0 - r)
        d_pi = (gic * s) * (1.0 - i)
        direct[at(j), :] = gi * s
        pair[at(j), pl.ds(0, width)] = d_pa
        pair[at(j), pl.ds(width, width)] = d_pi
        sum_r = sum_r + d_pa
        sum_i = sum_i + d_pi
        sum_d = sum_d + d_r
        past = state_ref[at(j), :]
    for n, total in enumerate((sum_r, sum_i, sum_d)):
        sums_ref[at(n), :] += total

    both = pair[...].astype(BF16)
    both_ref[...] = both
    direct[...] += contract_last(both, gates_ref[...])

    p1, p2, p3 = (edge_ref[at(k), :] for k in range(3))
    sums = [zero] * 5
    w = [par_ref[pl.ds(1 + k, 1), :] for k in range(4)]

    def behind(j, k):
        return bx_ref[at(j - k), :] if j >= k else ahead[at(k - j), :]

    for j in range(STEPS - 1, -1, -1):
        d = direct[at(j), :]
        m = mask_ref[at(j), :]
        d1, d2, d3 = (d * m[:, k : k + 1] for k in (1, 2, 3))
        direct[at(j), :] = w[0] * d + p1
        p1 = w[1] * d1 + p2
        p2 = w[2] * d2 + p3
        p3 = w[3] * d3
        for n, term in enumerate((d * behind(j, 0), d1 * behind(j, 1), d2 * behind(j, 2), d3 * behind(j, 3))):
            sums[n + 1] = sums[n + 1] + term
        sums[0] = sums[0] + d
    for n, total in enumerate(sums):
        sums_ref[at(3 + n), :] += total
    for k, p in enumerate((p1, p2, p3)):
        edge_ref[at(k), :] = p
    out_ref[...] = direct[...].astype(BF16)

    @pl.when(step_at == 0)
    def _():
        tail_ref[...] = direct[pl.ds(ROWS - 32, 32), :]


def gate_gradients(grad, reach, r, i, conv, state, both, masks, prev, ends, params, gates):
    tokens, width = grad.shape
    tiles = tokens // ROWS
    wide = wide_block(width, tiles)
    ahead = lambda n: pl.BlockSpec(
        (n, width), lambda t: (jnp.maximum((tiles - 1 - t) * (ROWS // n) - 1, 0), 0)
    )
    return pl.pallas_call(
        gate_grad_kernel,
        name="gate_gradients",
        grid=(tiles,),
        in_specs=[
            wide, wide, wide, wide, wide, wide, ahead(8), wide, ahead(32), wide_block(8, tiles),
            whole(prev), whole(ends), whole(params), whole(gates),
        ],
        out_specs=[
            wide, fixed(32, width), fixed(24, width), fixed(64, width), wide_block(2 * width, tiles),
        ],
        out_shape=[
            jax.ShapeDtypeStruct((tokens, width), BF16),
            jax.ShapeDtypeStruct((32, width), F32),
            jax.ShapeDtypeStruct((24, width), F32),
            jax.ShapeDtypeStruct((64, width), F32),
            jax.ShapeDtypeStruct((tokens, 2 * width), BF16),
        ],
        scratch_shapes=[
            pltpu.VMEM((ROWS, 2 * width), F32),
            pltpu.VMEM((ROWS, width), F32),
            pltpu.VMEM((32, width), F32),
        ],
        compiler_params=tile_params(),
        cost_estimate=pl.CostEstimate(
            flops=4 * grad.size * width, bytes_accessed=34 * grad.size,
            transcendentals=2 * grad.size,
        ),
    )(grad, reach, r, i, conv, state, state, both, both, masks, prev, ends, params, gates)


def settle_kernel(main_ref, tail_ref, edge_ref, beyond_ref, out_ref):
    del main_ref
    width = tail_ref.shape[1]
    row = lax.broadcasted_iota(jnp.int32, (8, width), 0)
    steps = [tail_ref[at(0), :]]
    for k in (2, 1, 0):
        up = pltpu.roll(edge_ref[at(k), :], 7, 0)
        up = jnp.where(row == 7, beyond_ref[pl.ds(k, 1), :], up)
        steps.append(tail_ref[at(3 - k), :] + up)
    out_ref[...] = jnp.concatenate(steps, axis=0).astype(BF16)


def settled(main, tail, edge, beyond):
    rows, width = tail.shape
    last = pl.BlockSpec((rows, width), lambda t: (main.shape[0] // rows - 1, 0))
    return pl.pallas_call(
        settle_kernel,
        name="settle",
        grid=(1,),
        in_specs=[last, whole(tail), whole(edge), whole(beyond)],
        out_specs=last,
        out_shape=jax.ShapeDtypeStruct(main.shape, main.dtype),
        input_output_aliases={0: 0},
        compiler_params=tile_params(),
        cost_estimate=pl.CostEstimate(flops=4 * tail.size, bytes_accessed=12 * tail.size, transcendentals=0),
    )(main, tail, edge, beyond)


def units_kernel(
    n2_ref, gate_ref, up_ref, d_hid_ref, hid_ref, d_gate_ref, d_up_ref, pull_ref
):
    tokens = n2_ref.shape[0]
    step_at = pl.program_id(0)
    rows = min(256, tokens)
    for t in range(tokens // rows):
        here = pl.ds(t * rows, rows)
        gate = dot(n2_ref[here, :], gate_ref[...])
        up = dot(n2_ref[here, :], up_ref[...])
        act, slope = gelu_parts(gate)
        d_hid = d_hid_ref[here, :]
        d_gate = (slope * up * d_hid).astype(BF16)
        d_up = (act * d_hid).astype(BF16)
        hid_ref[here, :] = (act * up).astype(BF16)
        d_gate_ref[here, :] = d_gate
        d_up_ref[here, :] = d_up
        pull = d_gate.astype(F32) * gate + d_up.astype(F32) * up
        pull = sum(pull[:, n : n + 128] for n in range(0, pull.shape[1], 128))

        @pl.when(step_at == 0)
        def _():
            pull_ref[here, :] = pull

        @pl.when(step_at > 0)
        def _():
            pull_ref[here, :] += pull


def mlp_units(n2, gate_weight, up_weight, d_hid):
    tokens, width = n2.shape
    units = d_hid.shape[1]
    each = 512 if units % 512 == 0 else 256
    column = lambda rows: pl.BlockSpec((rows, each), lambda j: (0, j))
    low = jax.ShapeDtypeStruct((tokens, units), BF16)
    return pl.pallas_call(
        units_kernel,
        name="mlp_units",
        grid=(units // each,),
        in_specs=[
            pl.BlockSpec((tokens, width), lambda j: (0, 0), pipeline_mode=pl.Buffered(1)),
            column(width), column(width), column(tokens),
        ],
        out_specs=[column(tokens)] * 3 + [pl.BlockSpec((tokens, 128), lambda j: (0, 0))],
        out_shape=[low, low, low, jax.ShapeDtypeStruct((tokens, 128), F32)],
        compiler_params=pltpu.CompilerParams(
            dimension_semantics=("arbitrary",), vmem_limit_bytes=48 << 20
        ),
        cost_estimate=pl.CostEstimate(
            flops=4 * tokens * width * units, transcendentals=tokens * units,
            bytes_accessed=2 * (tokens * width + 2 * width * units) + 10 * tokens * units,
        ),
    )(n2, gate_weight, up_weight, d_hid)


def pair_kernel(left_ref, right_ref, over_ref, under_ref, out_ref):
    out_ref[...] = (dot(left_ref[...], over_ref[...]) + dot(right_ref[...], under_ref[...])).astype(BF16)


def pair_product(left, right, over, under):
    tokens, depth = left.shape
    width = over.shape[1]
    rows = min(256, tokens)
    tall = lambda n: pl.BlockSpec((rows, n), lambda t: (t, 0))
    held = lambda a: pl.BlockSpec(a.shape, lambda t: (0, 0), pipeline_mode=pl.Buffered(1))
    return pl.pallas_call(
        pair_kernel,
        name="pair_product",
        grid=(tokens // rows,),
        in_specs=[tall(depth), tall(depth), held(over), held(under)],
        out_specs=tall(width),
        out_shape=jax.ShapeDtypeStruct((tokens, width), BF16),
        compiler_params=pltpu.CompilerParams(
            dimension_semantics=("arbitrary",), vmem_limit_bytes=32 << 20
        ),
        cost_estimate=pl.CostEstimate(
            flops=4 * tokens * depth * width, transcendentals=0,
            bytes_accessed=2 * (tokens * (2 * depth + width) + 2 * depth * width),
        ),
    )(left, right, over, under)


def shifted(x, axis, by):
    peers = lax.axis_size(axis)
    pairs = [(i, i + by) for i in range(peers) if 0 <= i + by < peers]
    return lax.ppermute(x, axis, pairs)


def bit_orders():
    bits = (lax.axis_size("seq") - 1).bit_length()
    outer = list(range(1, bits))
    return outer, outer[::-1]


def across(x, bit, axis="seq"):
    n = lax.axis_size(axis)
    return lax.ppermute(x, axis, [(i, i ^ (1 << bit)) for i in range(n)])


def own_bit(bit, axis="seq"):
    return (lax.axis_index(axis) >> bit) & 1


def relative(x, order, axis=1):
    n = lax.axis_size("seq")
    each = x.shape[axis] // n
    bits = len(order)
    out = []
    for place in range(n):
        number = sum(1 << bit for k, bit in enumerate(order) if place >> (bits - 1 - k) & 1)
        start = (lax.axis_index("seq") ^ number) * each
        out.append(lax.dynamic_slice_in_dim(x, start, each, axis))
    return jnp.concatenate(out, axis=axis)


def crossed(x, bit, axis):
    half = x.shape[axis] // 2
    give = lax.slice_in_dim(x, half, 2 * half, axis=axis).astype(BF16)
    keep = lax.slice_in_dim(x, 0, half, axis=axis).astype(F32)
    return keep + across(give, bit).astype(F32)


def exchanged(x, axis):
    n = lax.axis_size(axis)
    for bit in range((n - 1).bit_length()):
        x = x + across(x, bit, axis)
    return x


def places(order):
    n = lax.axis_size("seq")
    away = lax.axis_index("seq") ^ jnp.arange(n, dtype=jnp.int32)
    bits = len(order)
    return sum(((away >> bit) & 1) << (bits - 1 - k) for k, bit in enumerate(order))


def picked(routes, tables, fill, outs, name):
    n = lax.axis_size("seq")
    half = n // 2
    count = len(routes)

    def kernel(*refs):
        step_at = pl.program_id(0)
        sources, results = refs[count : 3 * count], refs[3 * count :]
        for side in range(count):
            near = refs[side][step_at] < half

            @pl.when(near)
            def _():
                fill(side, sources[2 * side], results)

            @pl.when(jnp.logical_not(near))
            def _():
                fill(side, sources[2 * side + 1], results)

    def pick(array, which, far):
        def block(s, *at):
            here, other = at[which][s], at[which][s ^ 1]
            return array[2](lax.rem(jnp.where((here >= half) == far, here, other), half))

        return pl.BlockSpec(array[1], block)

    return pl.pallas_call(
        kernel,
        name=name,
        grid_spec=pltpu.PrefetchScalarGridSpec(
            num_scalar_prefetch=count,
            grid=(n,),
            in_specs=[
                pick(array, side, far)
                for side, route in enumerate(routes)
                for far, array in enumerate(route)
            ],
            out_specs=[pl.BlockSpec(block, at) for _, block, at in outs],
        ),
        out_shape=[shape for shape, _, _ in outs],
        compiler_params=pltpu.CompilerParams(
            dimension_semantics=("arbitrary",), vmem_limit_bytes=40 << 20
        ),
        cost_estimate=pl.CostEstimate(
            flops=0, transcendentals=0,
            bytes_accessed=sum(a[0].size * 2 for r in routes for a in r)
            + sum(o[0].size * 4 for o in outs),
        ),
    )(*tables, *(a[0] for r in routes for a in r))


def ordered(routes, tables, outputs, name):
    n = lax.axis_size("seq")
    each = routes[0][0].shape[1] // (n // 2)
    wrap = lambda a: (a, (a.shape[0], each), lambda place: (0, place))

    def fill(side, ref, refs):
        for out, pieces in zip(refs, outputs):
            row = 0
            for route, start, rows in pieces:
                if route == side:
                    out[pl.ds(row, rows), :] = ref[pl.ds(start, rows), :].astype(F32)
                row += rows

    outs = []
    for pieces in outputs:
        rows = sum(piece[2] for piece in pieces)
        shape = jax.ShapeDtypeStruct((rows, n * each), F32)
        outs.append((shape, (rows, each), lambda s, *at: (0, s)))
    return picked([[wrap(a) for a in route] for route in routes], tables, fill, outs, name)


def joined(x, order):
    x = x[None]
    for bit in order:
        x = jnp.concatenate([x, across(x, bit)])
    return x


def mlp_weights(own_a, far_a, own_b, far_b, tables, lead):
    n = lax.axis_size("seq")
    units = own_a.shape[2]
    cut = own_a.shape[1] - lead
    wrap = lambda a: (a, (1, *a.shape[1:]), lambda place: (place, 0, 0))

    def fill(side, ref, refs):
        refs[side][0] = ref[0, pl.ds(0, lead), :]
        refs[2][0, side] = ref[0, pl.ds(lead, cut), :]

    full = (jax.ShapeDtypeStruct((n, lead, units), BF16), (1, lead, units), lambda s, *at: (s, 0, 0))
    down = (
        jax.ShapeDtypeStruct((n, 2, cut, units), BF16), (1, 2, cut, units),
        lambda s, *at: (s, 0, 0, 0),
    )
    routes = [[wrap(own_a), wrap(far_a)], [wrap(own_b), wrap(far_b)]]
    gate, up, down = picked(routes, tables, fill, [full, full, down], "mlp_weights")
    return gate.reshape(-1, units), up.reshape(-1, units), down.reshape(-1, units)


def output_rows(own_a, far_a, own_b, far_b, tables):
    n = lax.axis_size("seq")
    _, groups, part, middle = own_a.shape
    wrap = lambda a: (a, (1, *a.shape[1:]), lambda place: (place, 0, 0, 0))

    def fill(side, ref, refs):
        refs[0][:, 0, :, pl.ds(side * middle, middle)] = ref[0]

    out = (
        jax.ShapeDtypeStruct((groups, n, part, 2 * middle), BF16), (groups, 1, part, 2 * middle),
        lambda s, *at: (0, s, 0, 0),
    )
    routes = [[wrap(own_a), wrap(far_a)], [wrap(own_b), wrap(far_b)]]
    return picked(routes, tables, fill, [out], "output_rows")[0].reshape(-1, 2 * middle)


def chained(decays, values, place, reverse):
    devices, stretches = decays.shape[:2]
    total = jnp.zeros_like(values[0, 0])
    out = []
    hops = [(d, s) for d in range(devices) for s in range(stretches)]
    own_d = lax.dynamic_index_in_dim(decays, place, 0, False)
    own_v = lax.dynamic_index_in_dim(values, place, 0, False)
    order = range(stretches - 1, -1, -1) if reverse else range(stretches)
    whole_d, whole_v = [], []
    for d in range(devices):
        decay, value = jnp.ones_like(total), jnp.zeros_like(total)
        for s in order:
            value = values[d, s] + decays[d, s] * value
            decay = decay * decays[d, s]
        whole_d.append(decay)
        whole_v.append(value)
    for hop in range(devices - 1):
        d = devices - 1 - hop if reverse else hop
        live = d > place if reverse else d < place
        total = jnp.where(live, whole_v[d] + whole_d[d] * total, total)
    for s in order:
        out.append(total)
        total = own_v[s] + own_d[s] * total
    return jnp.stack(out[::-1] if reverse else out)


def gelu(y):
    return y * (0.5 + 0.5 * jnp.tanh(y * (GELU_C + (GELU_C * GELU_A) * (y * y))))


def side_by_side(x):
    rows = x.shape[0]
    return jnp.swapaxes(x.reshape(8, rows // 8, *x.shape[1:]), 0, 1).reshape(x.shape)


def in_order(x):
    rows = x.shape[0]
    return jnp.swapaxes(x.reshape(rows // 8, 8, *x.shape[1:]), 0, 1).reshape(x.shape)


def block_diagonal(blocks, padded):
    count, size, _ = blocks.shape
    rows = [
        jnp.pad(blocks[b], ((0, 0), (b * size, padded - (b + 1) * size))) for b in range(count)
    ]
    return jnp.pad(jnp.concatenate(rows, axis=0), ((0, padded - count * size), (0, 0)))


def after(value, *others):
    return lax.optimization_barrier((value, *others))[0]


def row_major(x):
    return with_layout_constraint(x, Layout(major_to_minor=tuple(range(x.ndim))))


def gather_features(x):
    return lax.all_gather(x, "tp", axis=1, tiled=True)


def scatter_features(x):
    return lax.psum_scatter(x.astype(BF16), "tp", scatter_dimension=1, tiled=True).astype(F32)


def on_device(
    hidden_in, segment_ids, first_gain, input_weight, gelu_weight, conv_weight, conv_bias,
    recur_gate, input_gate, recur_bias, input_bias, decay_param, output_weight, second_gain,
    gate_weight, up_weight, down_weight, grad_out,
):
    tokens, share = hidden_in.shape
    channels = input_weight.shape[1]
    padded = -(-channels // 128) * 128
    extra = padded - channels
    taps = conv_weight.shape[0]
    halo = taps - 1
    blocks, size = recur_gate.shape[0], recur_gate.shape[1]
    width = grad_out.shape[1]
    units = gate_weight.shape[1]
    seq_devices = lax.axis_size("seq")
    tp_devices = lax.axis_size("tp")
    seq_place = lax.axis_index("seq")
    share_start = lax.axis_index("tp") * share
    order_a, order_b = bit_orders()

    route_a, route_b = [0, *order_a], [0, *order_b]

    x_low = side_by_side(hidden_in)
    full = gather_features(x_low)

    down_t = down_weight.T
    lead = down_t.shape[0]
    cut = lead // 2
    legs = [
        (jnp.concatenate([gate_weight, down_t[:cut]]), order_a),
        (jnp.concatenate([up_weight, down_t[cut:]]), order_b),
    ]
    first = [joined(a, order[:-1]) for a, order in legs]
    (
        segment_ids, input_weight, gelu_weight, recur_gate, input_gate, output_weight, grad_out,
        *first,
    ) = lax.optimization_barrier(
        (segment_ids, input_weight, gelu_weight, recur_gate, input_gate, output_weight, grad_out, *first)
    )
    second = [across(a, order[-1]) for a, (_, order) in zip(first, legs)]
    part = channels // seq_devices
    own_rows = lax.dynamic_slice_in_dim(output_weight, seq_place * part, part, 0)

    ids = segment_ids.astype(F32)
    prev_ids = shifted(ids[tokens - halo :], "seq", 1)
    prev_ids = jnp.where(seq_place == 0, -1.0, prev_ids)
    next_id = jnp.where(seq_place == seq_devices - 1, -1.0, shifted(ids[:1], "seq", -1))
    ext = jnp.concatenate([prev_ids, ids])
    same = [(ext[halo - k : halo - k + tokens] == ids).astype(F32) for k in range(taps)]
    masks = side_by_side(jnp.stack(same + [jnp.zeros_like(ids)] * (8 - taps), axis=1))
    next_ids = jnp.concatenate([ids[1:], next_id])
    closing = (next_ids != ids).astype(F32)[None, :]
    member = (segment_ids[None, :] == jnp.arange(SEGS, dtype=jnp.int32)[:, None]).astype(F32)
    picks = side_by_side((member * closing).T).T

    slope = -DECAY_SCALE * jax.nn.softplus(-decay_param)
    params = jnp.concatenate(
        [jnp.stack([conv_bias]), conv_weight, jnp.stack([recur_bias, input_bias, slope])], axis=0
    )
    params = jnp.pad(params, ((0, 0), (0, extra)))
    gates = jnp.concatenate(
        [block_diagonal(recur_gate, padded), block_diagonal(input_gate, padded)], axis=1
    )
    pad_rows = lambda a: jnp.pad(a, ((0, extra), (0, 0)))
    input_padded, gelu_padded = pad_rows(input_weight.T), pad_rows(gelu_weight.T)
    branch_weight = jnp.concatenate([input_padded, gelu_padded], axis=0)
    output_padded = pad_rows(output_weight)
    grad_rows = side_by_side(grad_out)
    (
        params, gates, branch_weight, output_padded, grad_rows, masks, own_rows, full,
        input_padded, gelu_padded,
    ) = lax.optimization_barrier(
        (
            params, gates, branch_weight, output_padded, grad_rows, masks, own_rows, full,
            input_padded, gelu_padded,
        )
    )

    x = full.astype(F32)
    r1 = lax.rsqrt(jnp.mean(x * x, axis=1, keepdims=True) + EPSILON)
    n1 = (x * r1 * first_gain).astype(BF16)
    both = row_major(contract_last(n1, branch_weight))
    last = both[tokens - 8 * halo :, :padded].reshape(halo, 8, padded)
    before = shifted(last[:, 7], "seq", 1)
    prev = jnp.concatenate([before[:, None], last[:, :7]], axis=1).reshape(8 * halo, padded)
    over_tp = lax.all_gather(own_rows, "tp", axis=0, tiled=True)
    both, *second = lax.optimization_barrier((both, *second))
    conv, low, r, i, local, reach = forward_recurrence(both, prev, masks, params, gates)
    ends = jnp.stack([reach[tokens - 8 :], local[tokens - 8 :]])
    ends, over_tp = lax.optimization_barrier((ends, over_tp))
    ends = lax.all_gather(ends, "seq", axis=0)
    incoming = chained(ends[:, 0], ends[:, 1], seq_place, False)
    steps = lambda a: a.reshape(tokens // 8, 8, padded)
    state = (steps(local) + steps(reach) * incoming[None]).reshape(tokens, padded)
    mixed = (gelu(both[:, padded : padded + channels]) * state[:, :channels]).astype(BF16)
    mixed_full = lax.all_gather(mixed, "tp", axis=1, tiled=True)
    over_tp, _ = lax.optimization_barrier((over_tp, mixed))
    over_tp = over_tp.reshape(tp_devices, part, width)
    middle = width // 2
    rows_a = joined(over_tp[:, :, :middle], order_a)
    rows_b = joined(over_tp[:, :, middle:], order_b)
    grad_rows, *held = lax.optimization_barrier((grad_rows, *first, *second, mixed))
    own_a, own_b = (
        jnp.concatenate([held[leg], held[leg + len(legs)]]) for leg in range(len(legs))
    )
    tables = places([0, *order_a[::-1]]), places([0, *order_b[::-1]])
    gate_full, up_full, down_full = mlp_weights(
        own_a, across(own_a, 0), own_b, across(own_b, 0), tables, lead
    )
    d_hid = dot(grad_rows, down_full)
    output_full = output_rows(rows_a, across(rows_a, 0), rows_b, across(rows_b, 0), tables)
    d_hid, output_full, gate_full, up_full = lax.optimization_barrier(
        (d_hid, output_full, gate_full, up_full)
    )
    resid = x + dot(mixed_full, output_full)

    r2 = lax.rsqrt(jnp.mean(resid * resid, axis=1, keepdims=True) + EPSILON)
    n2 = (resid * r2 * second_gain).astype(BF16)
    resid_share = lax.dynamic_slice_in_dim(resid, share_start, share, 1)
    n2, resid_share = lax.optimization_barrier((n2, resid_share))
    hid, d_gate, d_up, pull2 = mlp_units(n2, gate_full, up_full, d_hid)
    d_n2_part = (contract_last(d_gate, gate_full) + contract_last(d_up, up_full)).astype(BF16)
    d_n2 = scatter_features(d_n2_part)
    n2_w, hid_w, pull2 = lax.optimization_barrier((n2, hid, pull2, d_n2_part))[:3]
    pull2 = lax.psum(jnp.sum(pull2, axis=1), "tp")
    grad_w = after(grad_rows, d_n2_part)
    grad_a, grad_b = relative(grad_w, route_a), relative(grad_w, route_b)
    half = units // 2
    n2_a, n2_b = relative(n2_w, route_a), relative(n2_w, route_b)
    products = [
        (n2_a, d_gate, order_a), (n2_b, d_up, order_b),
        (grad_a, hid_w[:, :half], order_a), (grad_b, hid_w[:, half:], order_b),
    ]
    middle = width // 2
    gives = [across(contract_first(l[:, middle:], r).astype(BF16), 0) for l, r, _ in products]
    sums2 = [
        contract_first(l[:, :middle], r) + give.astype(F32)
        for (l, r, _), give in zip(products, gives)
    ]
    d_n2, pull2, *sums2 = lax.optimization_barrier((d_n2, pull2, *sums2))
    pull2 = pull2[:, None]
    gain_share = lax.dynamic_slice_in_dim(second_gain, share_start, share)
    scaled = d_n2 * gain_share * r2
    scaled_low = scaled.astype(BF16)
    scaled_full = gather_features(scaled_low)
    hid_w, state_w, d_n2_w, n1_w, _, *sums2 = lax.optimization_barrier(
        (hid_w, state, d_n2, n1, scaled_low, *sums2)
    )
    n1_a, n1_b = relative(n1_w, route_a), relative(n1_w, route_b)
    finals = jnp.dot(picks, state_w, precision=lax.Precision.HIGHEST, preferred_element_type=F32)
    grad_second = jnp.sum(d_n2_w * resid_share * r2, axis=0)
    mlp = contract_last(hid_w, down_full).astype(BF16)
    for leg in range(len(order_a) - 1):
        sums2 = [crossed(v, order[leg], 0) for v, (_, _, order) in zip(sums2, products)]
    centre = r2 * r2 * pull2 * (1.0 / width)
    last_gives = [v[v.shape[0] // 2 :].astype(BF16) for v in sums2]
    kept2 = [v[: v.shape[0] // 2] for v in sums2]
    scaled_full, mlp, finals, grad_second, n1_a, n1_b, *last_gives = lax.optimization_barrier(
        (scaled_full, mlp, finals, grad_second, n1_a, n1_b, *last_gives)
    )
    mlp_sum = lax.psum_scatter(mlp, "tp", scatter_dimension=1, tiled=True)
    last_gives = [across(v, order[-1]) for v, (_, _, order) in zip(last_gives, products)]

    d_resid_low, grad_local, reach_back, dby, heads = reverse_recurrence(
        grad_rows, scaled_full, n2, r2 * pull2 * (1.0 / width), (1.0 / second_gain)[None],
        output_padded, both, r, state, masks, params,
    )
    back = lambda l, r: contract_first(l, r[:, middle:]).astype(BF16)
    front = lambda l, r: contract_first(l, r[:, :middle])

    def split(totals):
        half = totals[0].shape[1] // 2
        return [t[:, :half] for t in totals], [t[:, half:].astype(BF16) for t in totals]

    def sent(gives, orders, n):
        return [across(give, order[n]) for give, order in zip(gives, orders)]

    def met(keeps, fars):
        return [keep + far.astype(F32) for keep, far in zip(keeps, fars)]

    def returned(totals, orders, n):
        return [
            jnp.concatenate([t, across(t, order[n])], axis=1) for t, order in zip(totals, orders)
        ]

    orders = [order_a, order_b]
    last = len(order_a) - 1
    resid_a = relative(d_resid_low, route_a)
    gives = [back(mixed, resid_a), back(dby, n1_b)]
    heads, gives, last_gives = lax.optimization_barrier((heads, gives, last_gives))
    fars = [across(give, 0) for give in gives]
    outgoing = lax.all_gather(heads.reshape(2, 8, padded), "seq", axis=0)
    message = chained(outgoing[:, 1], outgoing[:, 0], seq_place, True)
    border = jnp.concatenate([incoming, message])
    keeps, gives = split(met([front(mixed, resid_a), front(dby, n1_b)], fars))
    border, gives, keeps = lax.optimization_barrier((border, gives, keeps))
    fars = sent(gives, orders, 0)
    d_main, tail, edge, sums, pair = gate_gradients(
        grad_local, reach_back, r, i, conv, state, both, masks, prev, border, params, gates
    )
    edge, fars, keeps = lax.optimization_barrier((edge, fars, keeps))
    beyond = shifted(edge.reshape(halo, 8, padded)[:, 0], "seq", -1)
    early = met(keeps, fars)
    for n in range(1, last):
        keeps, gives = split(early)
        early = met(keeps, sent(gives, orders, n))
    keeps, gives = split(early)
    fars = sent(gives, orders, last)
    dbx = settled(d_main, tail, edge, beyond)
    part_a = padded // 2
    gives = [back(dbx[:, :part_a], n1_a), back(dbx[:, part_a:], n1_b)]
    gives, dbx, fars = lax.optimization_barrier((gives, dbx, fars))
    far_in = [across(give, 0) for give in gives]
    early = [t.astype(BF16) for t in met(keeps, fars)]
    dbx, early = lax.optimization_barrier((dbx, early))
    early = returned(early, orders, last)
    d_n1_part = pair_product(dbx, dby, input_padded, gelu_padded)
    d_n1_part, mlp_sum = lax.optimization_barrier((d_n1_part, mlp_sum))
    d_n1 = scatter_features(d_n1_part)
    dbx, d_n1_w, early = lax.optimization_barrier((dbx, d_n1_part, early))
    for n in range(last - 1, -1, -1):
        early = returned(early, orders, n)
    early_parts = [(t, across(t, 0)) for t in early]

    totals = [front(dbx[:, :part_a], n1_a), front(dbx[:, part_a:], n1_b)]
    keeps, gives = split(met(totals, far_in))
    gives, pair, sums, d_n1_w = lax.optimization_barrier((gives, pair, sums, d_n1_w))
    totals = met(keeps, sent(gives, orders, 0))
    for n in range(1, last + 1):
        keeps, gives = split(totals)
        totals = met(keeps, sent(gives, orders, n))
    ready = totals = [t.astype(BF16) for t in totals]
    for n in range(last, 0, -1):
        totals = returned(totals, orders, n)
    far_in = sent(totals, orders, 0)
    near_in = totals

    first_part = jnp.sum(d_n1_w.astype(F32) * n1.astype(F32), axis=0) / first_gain
    pull1 = jnp.sum(d_n1_w.astype(F32) * n1.astype(F32), axis=1)
    second_part = lax.dynamic_update_slice(jnp.zeros((width,), F32), grad_second, (share_start,))
    over_tp = exchanged(jnp.concatenate([pull1, first_part, second_part]), "tp")
    pull1, gains = over_tp[:tokens, None], over_tp[tokens:]
    gate_grads = contract_first(low, pair)
    corner = lambda n, b: gate_grads[
        b * size : (b + 1) * size, n * padded + b * size : n * padded + (b + 1) * size
    ]
    corners = jnp.concatenate([corner(n, b) for b in range(blocks) for n in (0, 1)], axis=1)
    corners = jnp.pad(corners, ((0, 0), (0, width - corners.shape[1])))
    sums = jnp.sum(sums.reshape(8, 8, padded), axis=1)
    small = jnp.concatenate([sums, finals], axis=0)[:, :channels]
    packed = jnp.concatenate([gains, small.reshape(-1)])
    packed = jnp.pad(packed, (0, -packed.size % (8 * width))).reshape(-1, width)
    few = packed.shape[0]
    extras = [relative(jnp.concatenate([corners, packed]), route_b)]
    keeps, gives = split(extras)
    extras = met(keeps, [across(gives[0], 0)])
    for n in range(last + 1):
        keeps, gives = split(extras)
        extras = met(keeps, sent(gives, [order_b], n))
    extras = [t.astype(BF16) for t in extras]

    kept2, last_gives, mlp_sum, resid_out = lax.optimization_barrier(
        (kept2, last_gives, mlp_sum, resid_share, gives)
    )[:4]
    d_n1, resid_share = lax.optimization_barrier((d_n1, resid_share, ready))[:2]
    done2 = [v + give.astype(F32) for v, give in zip(kept2, last_gives)]
    grad_gate_weight, grad_up_weight = done2[:2]
    grad_down_weight = jnp.concatenate(done2[2:], axis=1).T
    g_share = lax.dynamic_slice_in_dim(grad_rows, share_start, share, 1).astype(F32)
    d_resid_share = g_share + scaled - resid_share * centre
    block_out = in_order((resid_out + mlp_sum.astype(F32)).astype(BF16))
    gain1_share = lax.dynamic_slice_in_dim(first_gain, share_start, share)
    grad_in = (
        d_resid_share
        + d_n1 * gain1_share * r1
        - x_low.astype(F32) * (r1 * r1 * pull1 * (1.0 / width))
    )
    grad_in = in_order(grad_in.astype(BF16))
    outputs = (block_out, grad_gate_weight, grad_up_weight, grad_down_weight)
    for n in range(last, -1, -1):
        extras = returned(extras, [order_b], n)
    extra_parts = [(t, across(t, 0)) for t in extras]
    tables = places(route_a), places(route_b)
    early_grads = ordered(
        early_parts, tables, [[(0, 0, channels)], [(1, 0, channels)]], "early_gradients"
    )
    far_in, outputs, early_grads = lax.optimization_barrier((far_in, outputs, early_grads))
    grad_output_weight, grad_gelu = early_grads
    totals = [jnp.concatenate(both_ways, axis=1) for both_ways in zip(near_in, far_in)]
    far_in = [across(t, 0) for t in totals]
    far_in, extra_parts, grad_in = lax.optimization_barrier((far_in, extra_parts, grad_in))
    in_parts = list(zip(totals, far_in))
    block_out, grad_gate_weight, grad_up_weight, grad_down_weight = outputs
    grad_input, corners, packed = ordered(
        in_parts + extra_parts,
        (*tables, tables[1]),
        [[(0, 0, part_a), (1, 0, channels - part_a)], [(2, 0, size)], [(2, size, few)]],
        "last_gradients",
    )
    packed = packed.reshape(-1)
    gains = packed[: 2 * width]
    small = packed[2 * width : 2 * width + small.size].reshape(small.shape)
    corner_of = lambda n: jnp.stack(
        [corners[:, (2 * b + n) * size : (2 * b + n + 1) * size] for b in range(blocks)]
    )
    grad_decay = small[2] * (DECAY_SCALE * jax.nn.sigmoid(-decay_param))
    return (
        block_out,
        grad_in,
        gains[:width],
        grad_input.T,
        grad_gelu.T,
        small[4:8],
        small[3],
        corner_of(0),
        corner_of(1),
        small[0],
        small[1],
        grad_decay,
        grad_output_weight,
        gains[width:],
        grad_gate_weight,
        grad_up_weight,
        grad_down_weight,
        small[8:],
    )


def solution(mesh):
    row = P("tp")
    return jax.shard_map(
        on_device,
        mesh=mesh,
        in_specs=(
            P("seq", "tp"), P("seq"), P(), P(None, "tp"), P(None, "tp"), P(None, "tp"), row,
            P("tp", None, None), P("tp", None, None), row, row, row, P("tp", None), P(),
            P("seq", "tp"), P("seq", "tp"), P("tp", "seq"), P("seq", None),
        ),
        out_specs=(
            P("seq", "tp"), P("seq", "tp"), P(), P(None, "tp"), P(None, "tp"), P(None, "tp"), row,
            P("tp", None, None), P("tp", None, None), row, row, row, P("tp", None), P(),
            P("seq", "tp"), P("seq", "tp"), P("tp", "seq"), P(None, "tp"),
        ),
        check_vma=False,
    )
```

```python
import jax
import jax.numpy as jnp
from jax import lax
from jax.experimental import pallas as pl
from jax.experimental.layout import Layout, with_layout_constraint
from jax.experimental.pallas import tpu as pltpu
from jax.sharding import PartitionSpec as P

SEGS = 8
EPSILON = 1e-06
DECAY_SCALE = 8.0
GELU_C = 0.7978845608028654
GELU_A = 0.044715
F32 = jnp.float32
BF16 = jnp.bfloat16
VMEM_LIMIT = 58 << 20
STEPS = 16
ROWS = 8 * STEPS


def dot(left, right):
    return jnp.dot(left, right, preferred_element_type=F32)


def contract_first(left, right):
    return lax.dot_general(left, right, (((0,), (0,)), ((), ())), preferred_element_type=F32)


def contract_last(left, right):
    return lax.dot_general(left, right, (((1,), (1,)), ((), ())), preferred_element_type=F32)


def gelu_parts(y):
    y2 = y * y
    t = jnp.tanh(y * (GELU_C + (GELU_C * GELU_A) * y2))
    half = 0.5 + 0.5 * t
    slope = half + (0.5 * y) * (1.0 - t * t) * (GELU_C + (3.0 * GELU_C * GELU_A) * y2)
    return y * half, slope


def retained(log_decay, carried):
    y = 2.0 * log_decay
    series = -y * (1.0 + y * (1 / 2 + y * (1 / 6 + y * (1 / 24 + y * (1 / 120)))))
    return jnp.maximum(jnp.where(y > -0.0625, series, 1.0 - carried * carried), 1e-36)


def at(j):
    return pl.ds(8 * j, 8)


def tile_params():
    return pltpu.CompilerParams(dimension_semantics=("arbitrary",), vmem_limit_bytes=VMEM_LIMIT)


def wide_block(width, tiles=None, column=0):
    row = (lambda t: t) if tiles is None else (lambda t: tiles - 1 - t)
    return pl.BlockSpec((ROWS, width), lambda t: (row(t), column))


def whole(a):
    return pl.BlockSpec(a.shape, lambda t: (0,) * a.ndim)


def fixed(*dims):
    return pl.BlockSpec(dims, lambda t: (0,) * len(dims))


def forward_kernel(
    bx_ref, prev_ref, mask_ref, par_ref, gates_ref,
    conv_ref, low_ref, r_ref, i_ref, state_ref, decay_ref,
    lags, pre, carry,
):
    width = bx_ref.shape[1]

    @pl.when(pl.program_id(0) == 0)
    def _():
        lags[...] = prev_ref[...]
        carry[at(0), :] = jnp.zeros((8, width), F32)
        carry[at(1), :] = jnp.ones((8, width), F32)

    past = [lags[at(2 - k), :] for k in range(3)]
    for j in range(STEPS):
        now = bx_ref[at(j), :]
        m = mask_ref[at(j), :]
        out = par_ref[pl.ds(0, 1), :] + par_ref[pl.ds(1, 1), :] * now
        for k in range(3):
            out = out + par_ref[pl.ds(2 + k, 1), :] * (past[k] * m[:, k + 1 : k + 2])
        conv_ref[at(j), :] = out
        past = [now, past[0], past[1]]
    for k in range(3):
        lags[at(2 - k), :] = past[k]
    low = conv_ref[...].astype(BF16)
    low_ref[...] = low
    pre[...] = jnp.dot(low, gates_ref[...], preferred_element_type=F32)

    state, decay = carry[at(0), :], carry[at(1), :]
    for j in range(STEPS):
        live = jnp.broadcast_to(mask_ref[at(j), :][:, 1:2], state.shape) != 0.0
        r = 1.0 / (1.0 + jnp.exp(-(pre[at(j), pl.ds(0, width)] + par_ref[pl.ds(5, 1), :])))
        i = 0.5 + 0.5 * jnp.tanh(
            0.5 * (pre[at(j), pl.ds(width, width)] + par_ref[pl.ds(6, 1), :])
        )
        log_decay = par_ref[pl.ds(7, 1), :] * r
        a = jnp.exp(log_decay)
        e = retained(log_decay, a)
        drive = jnp.where(live, e * lax.rsqrt(e), 1.0) * (i * conv_ref[at(j), :])
        a = jnp.where(live, a, 0.0)
        state = a * state + drive
        decay = a * decay
        r_ref[at(j), :] = r
        i_ref[at(j), :] = i
        state_ref[at(j), :] = state
        decay_ref[at(j), :] = decay
    carry[at(0), :] = state
    carry[at(1), :] = decay


def forward_recurrence(both, prev, masks, params, gates):
    tokens, width = both.shape[0], prev.shape[1]
    size = tokens * width
    wide = wide_block(width)
    shape = lambda d: jax.ShapeDtypeStruct((tokens, width), d)
    return pl.pallas_call(
        forward_kernel,
        name="forward_recurrence",
        grid=(tokens // ROWS,),
        in_specs=[
            wide, whole(prev), pl.BlockSpec((ROWS, 8), lambda t: (t, 0)), whole(params),
            whole(gates),
        ],
        out_specs=[wide] * 6,
        out_shape=[shape(F32), shape(BF16), shape(F32), shape(F32), shape(F32), shape(F32)],
        scratch_shapes=[
            pltpu.VMEM((24, width), F32),
            pltpu.VMEM((ROWS, 2 * width), F32),
            pltpu.VMEM((16, width), F32),
        ],
        compiler_params=tile_params(),
        cost_estimate=pl.CostEstimate(
            flops=4 * size * width, bytes_accessed=30 * size, transcendentals=6 * size
        ),
    )(both, prev, masks, params, gates)


def reverse_kernel(
    grad_in_ref, scaled_ref, n2_ref, factor_ref, gain_ref, weight_ref, by_ref, r_ref, state_ref,
    mask_ref, par_ref,
    resid_ref, grad_ref, reach_ref, dby_ref, head_ref,
    dm, slopes,
):
    width = by_ref.shape[1]

    @pl.when(pl.program_id(0) == 0)
    def _():
        head_ref[at(0), :] = jnp.zeros((8, width), F32)
        head_ref[at(1), :] = jnp.ones((8, width), F32)

    centred = (n2_ref[...].astype(F32) * gain_ref[...]) * factor_ref[...]
    d_resid = grad_in_ref[...].astype(F32) + scaled_ref[...].astype(F32) - centred
    d_resid = d_resid.astype(BF16)
    resid_ref[...] = d_resid
    dm[...] = contract_last(d_resid, weight_ref[...])

    u, reach = head_ref[at(0), :], head_ref[at(1), :]
    for j in range(STEPS - 1, -1, -1):
        d = dm[at(j), :]
        act, slope = gelu_parts(by_ref[at(j), :])
        slopes[at(j), :] = slope * (state_ref[at(j), :] * d)
        live = jnp.broadcast_to(mask_ref[at(j), :][:, 1:2], u.shape) != 0.0
        a = jnp.where(live, jnp.exp(par_ref[pl.ds(7, 1), :] * r_ref[at(j), :]), 0.0)
        g = d * act + u
        grad_ref[at(j), :] = g
        reach_ref[at(j), :] = reach
        u = a * g
        reach = a * reach
    head_ref[at(0), :] = u
    head_ref[at(1), :] = reach
    dby_ref[...] = slopes[...].astype(BF16)


def reverse_recurrence(grad_rows, scaled, n2, factor, gain, weight, both, r, state, masks, params):
    tokens, full = grad_rows.shape
    width = weight.shape[0]
    tiles = tokens // ROWS
    wide = wide_block(width, tiles)
    whole_row = wide_block(full, tiles)
    shape = lambda n, d: jax.ShapeDtypeStruct((tokens, n), d)
    return pl.pallas_call(
        reverse_kernel,
        name="reverse_recurrence",
        grid=(tiles,),
        in_specs=[
            whole_row, whole_row, whole_row, wide_block(1, tiles), whole(gain), whole(weight),
            wide_block(width, tiles, 1), wide, wide, wide_block(8, tiles), whole(params),
        ],
        out_specs=[whole_row, wide, wide, wide, fixed(16, width)],
        out_shape=[
            shape(full, BF16), shape(width, F32), shape(width, F32), shape(width, BF16),
            jax.ShapeDtypeStruct((16, width), F32),
        ],
        scratch_shapes=[pltpu.VMEM((ROWS, width), F32), pltpu.VMEM((ROWS, width), F32)],
        compiler_params=tile_params(),
        cost_estimate=pl.CostEstimate(
            flops=2 * tokens * width * full, bytes_accessed=tokens * (8 * full + 24 * width),
            transcendentals=2 * tokens * width,
        ),
    )(grad_rows, scaled, n2, factor, gain, weight, both, r, state, masks, params)


def gate_grad_kernel(
    grad_ref, reach_ref, r_ref, i_ref, conv_ref, state_ref, before_ref, bx_ref, bx_before_ref,
    mask_ref, prev_ref, ends_ref, par_ref, gates_ref,
    out_ref, tail_ref, edge_ref, sums_ref, both_ref,
    pair, direct, ahead,
):
    width = grad_ref.shape[1]
    step_at = pl.program_id(0)
    first = step_at == pl.num_programs(0) - 1

    @pl.when(step_at == 0)
    def _():
        sums_ref[...] = jnp.zeros_like(sums_ref)
        edge_ref[...] = jnp.zeros_like(edge_ref)

    @pl.when(first)
    def _():
        ahead[at(0), :] = ends_ref[at(0), :]
        for k in range(3):
            ahead[at(1 + k), :] = prev_ref[at(2 - k), :]

    @pl.when(jnp.logical_not(first))
    def _():
        ahead[at(0), :] = before_ref[...]
        for k in range(3):
            ahead[at(1 + k), :] = bx_before_ref[at(3 - k), :]

    message = ends_ref[at(1), :]
    zero = jnp.zeros((8, width), F32)
    sum_r = sum_i = sum_d = zero
    slope = par_ref[pl.ds(7, 1), :]
    past = ahead[at(0), :]
    for j in range(STEPS):
        g = grad_ref[at(j), :] + reach_ref[at(j), :] * message
        r, i, conv = r_ref[at(j), :], i_ref[at(j), :], conv_ref[at(j), :]
        live = jnp.broadcast_to(mask_ref[at(j), :][:, 1:2], g.shape) != 0.0
        log_decay = slope * r
        a = jnp.exp(log_decay)
        e = retained(log_decay, a)
        inv = lax.rsqrt(e)
        s = jnp.where(live, e * inv, 1.0)
        gi = g * i
        gic = gi * conv
        d_log = jnp.where(live, a * (g * past - gic * (a * inv)), 0.0)
        d_r = d_log * r
        d_pa = (slope * d_r) * (1.0 - r)
        d_pi = (gic * s) * (1.0 - i)
        direct[at(j), :] = gi * s
        pair[at(j), pl.ds(0, width)] = d_pa
        pair[at(j), pl.ds(width, width)] = d_pi
        sum_r = sum_r + d_pa
        sum_i = sum_i + d_pi
        sum_d = sum_d + d_r
        past = state_ref[at(j), :]
    for n, total in enumerate((sum_r, sum_i, sum_d)):
        sums_ref[at(n), :] += total

    both = pair[...].astype(BF16)
    both_ref[...] = both
    direct[...] += contract_last(both, gates_ref[...])

    p1, p2, p3 = (edge_ref[at(k), :] for k in range(3))
    sums = [zero] * 5
    w = [par_ref[pl.ds(1 + k, 1), :] for k in range(4)]

    def behind(j, k):
        return bx_ref[at(j - k), :] if j >= k else ahead[at(k - j), :]

    for j in range(STEPS - 1, -1, -1):
        d = direct[at(j), :]
        m = mask_ref[at(j), :]
        d1, d2, d3 = (d * m[:, k : k + 1] for k in (1, 2, 3))
        direct[at(j), :] = w[0] * d + p1
        p1 = w[1] * d1 + p2
        p2 = w[2] * d2 + p3
        p3 = w[3] * d3
        for n, term in enumerate((d * behind(j, 0), d1 * behind(j, 1), d2 * behind(j, 2), d3 * behind(j, 3))):
            sums[n + 1] = sums[n + 1] + term
        sums[0] = sums[0] + d
    for n, total in enumerate(sums):
        sums_ref[at(3 + n), :] += total
    for k, p in enumerate((p1, p2, p3)):
        edge_ref[at(k), :] = p
    out_ref[...] = direct[...].astype(BF16)

    @pl.when(step_at == 0)
    def _():
        tail_ref[...] = direct[pl.ds(ROWS - 32, 32), :]


def gate_gradients(grad, reach, r, i, conv, state, both, masks, prev, ends, params, gates):
    tokens, width = grad.shape
    tiles = tokens // ROWS
    wide = wide_block(width, tiles)
    ahead = lambda n: pl.BlockSpec(
        (n, width), lambda t: (jnp.maximum((tiles - 1 - t) * (ROWS // n) - 1, 0), 0)
    )
    return pl.pallas_call(
        gate_grad_kernel,
        name="gate_gradients",
        grid=(tiles,),
        in_specs=[
            wide, wide, wide, wide, wide, wide, ahead(8), wide, ahead(32), wide_block(8, tiles),
            whole(prev), whole(ends), whole(params), whole(gates),
        ],
        out_specs=[
            wide, fixed(32, width), fixed(24, width), fixed(64, width), wide_block(2 * width, tiles),
        ],
        out_shape=[
            jax.ShapeDtypeStruct((tokens, width), BF16),
            jax.ShapeDtypeStruct((32, width), F32),
            jax.ShapeDtypeStruct((24, width), F32),
            jax.ShapeDtypeStruct((64, width), F32),
            jax.ShapeDtypeStruct((tokens, 2 * width), BF16),
        ],
        scratch_shapes=[
            pltpu.VMEM((ROWS, 2 * width), F32),
            pltpu.VMEM((ROWS, width), F32),
            pltpu.VMEM((32, width), F32),
        ],
        compiler_params=tile_params(),
        cost_estimate=pl.CostEstimate(
            flops=4 * grad.size * width, bytes_accessed=34 * grad.size,
            transcendentals=2 * grad.size,
        ),
    )(grad, reach, r, i, conv, state, state, both, both, masks, prev, ends, params, gates)


def settle_kernel(main_ref, tail_ref, edge_ref, beyond_ref, out_ref):
    del main_ref
    width = tail_ref.shape[1]
    row = lax.broadcasted_iota(jnp.int32, (8, width), 0)
    steps = [tail_ref[at(0), :]]
    for k in (2, 1, 0):
        up = pltpu.roll(edge_ref[at(k), :], 7, 0)
        up = jnp.where(row == 7, beyond_ref[pl.ds(k, 1), :], up)
        steps.append(tail_ref[at(3 - k), :] + up)
    out_ref[...] = jnp.concatenate(steps, axis=0).astype(BF16)


def settled(main, tail, edge, beyond):
    rows, width = tail.shape
    last = pl.BlockSpec((rows, width), lambda t: (main.shape[0] // rows - 1, 0))
    return pl.pallas_call(
        settle_kernel,
        name="settle",
        grid=(1,),
        in_specs=[last, whole(tail), whole(edge), whole(beyond)],
        out_specs=last,
        out_shape=jax.ShapeDtypeStruct(main.shape, main.dtype),
        input_output_aliases={0: 0},
        compiler_params=tile_params(),
        cost_estimate=pl.CostEstimate(flops=4 * tail.size, bytes_accessed=12 * tail.size, transcendentals=0),
    )(main, tail, edge, beyond)


def units_kernel(
    n2_ref, gate_ref, up_ref, d_hid_ref, hid_ref, d_gate_ref, d_up_ref, pull_ref
):
    tokens = n2_ref.shape[0]
    step_at = pl.program_id(0)
    rows = min(256, tokens)
    for t in range(tokens // rows):
        here = pl.ds(t * rows, rows)
        gate = dot(n2_ref[here, :], gate_ref[...])
        up = dot(n2_ref[here, :], up_ref[...])
        act, slope = gelu_parts(gate)
        d_hid = d_hid_ref[here, :]
        d_gate = (slope * up * d_hid).astype(BF16)
        d_up = (act * d_hid).astype(BF16)
        hid_ref[here, :] = (act * up).astype(BF16)
        d_gate_ref[here, :] = d_gate
        d_up_ref[here, :] = d_up
        pull = d_gate.astype(F32) * gate + d_up.astype(F32) * up
        pull = sum(pull[:, n : n + 128] for n in range(0, pull.shape[1], 128))

        @pl.when(step_at == 0)
        def _():
            pull_ref[here, :] = pull

        @pl.when(step_at > 0)
        def _():
            pull_ref[here, :] += pull


def mlp_units(n2, gate_weight, up_weight, d_hid):
    tokens, width = n2.shape
    units = d_hid.shape[1]
    each = 512 if units % 512 == 0 else 256
    column = lambda rows: pl.BlockSpec((rows, each), lambda j: (0, j))
    low = jax.ShapeDtypeStruct((tokens, units), BF16)
    return pl.pallas_call(
        units_kernel,
        name="mlp_units",
        grid=(units // each,),
        in_specs=[
            pl.BlockSpec((tokens, width), lambda j: (0, 0), pipeline_mode=pl.Buffered(1)),
            column(width), column(width), column(tokens),
        ],
        out_specs=[column(tokens)] * 3 + [pl.BlockSpec((tokens, 128), lambda j: (0, 0))],
        out_shape=[low, low, low, jax.ShapeDtypeStruct((tokens, 128), F32)],
        compiler_params=pltpu.CompilerParams(
            dimension_semantics=("arbitrary",), vmem_limit_bytes=48 << 20
        ),
        cost_estimate=pl.CostEstimate(
            flops=4 * tokens * width * units, transcendentals=tokens * units,
            bytes_accessed=2 * (tokens * width + 2 * width * units) + 10 * tokens * units,
        ),
    )(n2, gate_weight, up_weight, d_hid)


def pair_kernel(left_ref, right_ref, over_ref, under_ref, out_ref):
    out_ref[...] = (dot(left_ref[...], over_ref[...]) + dot(right_ref[...], under_ref[...])).astype(BF16)


def pair_product(left, right, over, under):
    tokens, depth = left.shape
    width = over.shape[1]
    rows = min(256, tokens)
    tall = lambda n: pl.BlockSpec((rows, n), lambda t: (t, 0))
    held = lambda a: pl.BlockSpec(a.shape, lambda t: (0, 0), pipeline_mode=pl.Buffered(1))
    return pl.pallas_call(
        pair_kernel,
        name="pair_product",
        grid=(tokens // rows,),
        in_specs=[tall(depth), tall(depth), held(over), held(under)],
        out_specs=tall(width),
        out_shape=jax.ShapeDtypeStruct((tokens, width), BF16),
        compiler_params=pltpu.CompilerParams(
            dimension_semantics=("arbitrary",), vmem_limit_bytes=32 << 20
        ),
        cost_estimate=pl.CostEstimate(
            flops=4 * tokens * depth * width, transcendentals=0,
            bytes_accessed=2 * (tokens * (2 * depth + width) + 2 * depth * width),
        ),
    )(left, right, over, under)


def shifted(x, axis, by):
    peers = lax.axis_size(axis)
    pairs = [(i, i + by) for i in range(peers) if 0 <= i + by < peers]
    return lax.ppermute(x, axis, pairs)


def bit_orders():
    bits = (lax.axis_size("seq") - 1).bit_length()
    outer = list(range(1, bits))
    return outer, outer[::-1]


def across(x, bit, axis="seq"):
    n = lax.axis_size(axis)
    return lax.ppermute(x, axis, [(i, i ^ (1 << bit)) for i in range(n)])


def own_bit(bit, axis="seq"):
    return (lax.axis_index(axis) >> bit) & 1


def relative(x, order, axis=1):
    n = lax.axis_size("seq")
    each = x.shape[axis] // n
    bits = len(order)
    out = []
    for place in range(n):
        number = sum(1 << bit for k, bit in enumerate(order) if place >> (bits - 1 - k) & 1)
        start = (lax.axis_index("seq") ^ number) * each
        out.append(lax.dynamic_slice_in_dim(x, start, each, axis))
    return jnp.concatenate(out, axis=axis)


def crossed(x, bit, axis):
    half = x.shape[axis] // 2
    give = lax.slice_in_dim(x, half, 2 * half, axis=axis).astype(BF16)
    keep = lax.slice_in_dim(x, 0, half, axis=axis).astype(F32)
    return keep + across(give, bit).astype(F32)


def exchanged(x, axis):
    n = lax.axis_size(axis)
    for bit in range((n - 1).bit_length()):
        x = x + across(x, bit, axis)
    return x


def places(order):
    n = lax.axis_size("seq")
    away = lax.axis_index("seq") ^ jnp.arange(n, dtype=jnp.int32)
    bits = len(order)
    return sum(((away >> bit) & 1) << (bits - 1 - k) for k, bit in enumerate(order))


def picked(routes, tables, fill, outs, name):
    n = lax.axis_size("seq")
    half = n // 2
    count = len(routes)

    def kernel(*refs):
        step_at = pl.program_id(0)
        sources, results = refs[count : 3 * count], refs[3 * count :]
        for side in range(count):
            near = refs[side][step_at] < half

            @pl.when(near)
            def _():
                fill(side, sources[2 * side], results)

            @pl.when(jnp.logical_not(near))
            def _():
                fill(side, sources[2 * side + 1], results)

    def pick(array, which, far):
        def block(s, *at):
            here, other = at[which][s], at[which][s ^ 1]
            return array[2](lax.rem(jnp.where((here >= half) == far, here, other), half))

        return pl.BlockSpec(array[1], block)

    return pl.pallas_call(
        kernel,
        name=name,
        grid_spec=pltpu.PrefetchScalarGridSpec(
            num_scalar_prefetch=count,
            grid=(n,),
            in_specs=[
                pick(array, side, far)
                for side, route in enumerate(routes)
                for far, array in enumerate(route)
            ],
            out_specs=[pl.BlockSpec(block, at) for _, block, at in outs],
        ),
        out_shape=[shape for shape, _, _ in outs],
        compiler_params=pltpu.CompilerParams(
            dimension_semantics=("arbitrary",), vmem_limit_bytes=40 << 20
        ),
        cost_estimate=pl.CostEstimate(
            flops=0, transcendentals=0,
            bytes_accessed=sum(a[0].size * 2 for r in routes for a in r)
            + sum(o[0].size * 4 for o in outs),
        ),
    )(*tables, *(a[0] for r in routes for a in r))


def ordered(routes, tables, outputs, name):
    n = lax.axis_size("seq")
    each = routes[0][0].shape[1] // (n // 2)
    wrap = lambda a: (a, (a.shape[0], each), lambda place: (0, place))

    def fill(side, ref, refs):
        for out, pieces in zip(refs, outputs):
            row = 0
            for route, start, rows in pieces:
                if route == side:
                    out[pl.ds(row, rows), :] = ref[pl.ds(start, rows), :].astype(F32)
                row += rows

    outs = []
    for pieces in outputs:
        rows = sum(piece[2] for piece in pieces)
        shape = jax.ShapeDtypeStruct((rows, n * each), F32)
        outs.append((shape, (rows, each), lambda s, *at: (0, s)))
    return picked([[wrap(a) for a in route] for route in routes], tables, fill, outs, name)


def joined(x, order):
    x = x[None]
    for bit in order:
        x = jnp.concatenate([x, across(x, bit)])
    return x


def mlp_weights(own_a, far_a, own_b, far_b, tables, lead):
    n = lax.axis_size("seq")
    units = own_a.shape[2]
    cut = own_a.shape[1] - lead
    wrap = lambda a: (a, (1, *a.shape[1:]), lambda place: (place, 0, 0))

    def fill(side, ref, refs):
        refs[side][0] = ref[0, pl.ds(0, lead), :]
        refs[2][0, side] = ref[0, pl.ds(lead, cut), :]

    full = (jax.ShapeDtypeStruct((n, lead, units), BF16), (1, lead, units), lambda s, *at: (s, 0, 0))
    down = (
        jax.ShapeDtypeStruct((n, 2, cut, units), BF16), (1, 2, cut, units),
        lambda s, *at: (s, 0, 0, 0),
    )
    routes = [[wrap(own_a), wrap(far_a)], [wrap(own_b), wrap(far_b)]]
    gate, up, down = picked(routes, tables, fill, [full, full, down], "mlp_weights")
    return gate.reshape(-1, units), up.reshape(-1, units), down.reshape(-1, units)


def output_rows(own_a, far_a, own_b, far_b, tables):
    n = lax.axis_size("seq")
    _, groups, part, middle = own_a.shape
    wrap = lambda a: (a, (1, *a.shape[1:]), lambda place: (place, 0, 0, 0))

    def fill(side, ref, refs):
        refs[0][:, 0, :, pl.ds(side * middle, middle)] = ref[0]

    out = (
        jax.ShapeDtypeStruct((groups, n, part, 2 * middle), BF16), (groups, 1, part, 2 * middle),
        lambda s, *at: (0, s, 0, 0),
    )
    routes = [[wrap(own_a), wrap(far_a)], [wrap(own_b), wrap(far_b)]]
    return picked(routes, tables, fill, [out], "output_rows")[0].reshape(-1, 2 * middle)


def chained(decays, values, place, reverse):
    devices, stretches = decays.shape[:2]
    total = jnp.zeros_like(values[0, 0])
    out = []
    hops = [(d, s) for d in range(devices) for s in range(stretches)]
    own_d = lax.dynamic_index_in_dim(decays, place, 0, False)
    own_v = lax.dynamic_index_in_dim(values, place, 0, False)
    order = range(stretches - 1, -1, -1) if reverse else range(stretches)
    whole_d, whole_v = [], []
    for d in range(devices):
        decay, value = jnp.ones_like(total), jnp.zeros_like(total)
        for s in order:
            value = values[d, s] + decays[d, s] * value
            decay = decay * decays[d, s]
        whole_d.append(decay)
        whole_v.append(value)
    for hop in range(devices - 1):
        d = devices - 1 - hop if reverse else hop
        live = d > place if reverse else d < place
        total = jnp.where(live, whole_v[d] + whole_d[d] * total, total)
    for s in order:
        out.append(total)
        total = own_v[s] + own_d[s] * total
    return jnp.stack(out[::-1] if reverse else out)


def gelu(y):
    return y * (0.5 + 0.5 * jnp.tanh(y * (GELU_C + (GELU_C * GELU_A) * (y * y))))


def side_by_side(x):
    rows = x.shape[0]
    return jnp.swapaxes(x.reshape(8, rows // 8, *x.shape[1:]), 0, 1).reshape(x.shape)


def in_order(x):
    rows = x.shape[0]
    return jnp.swapaxes(x.reshape(rows // 8, 8, *x.shape[1:]), 0, 1).reshape(x.shape)


def block_diagonal(blocks, padded):
    count, size, _ = blocks.shape
    rows = [
        jnp.pad(blocks[b], ((0, 0), (b * size, padded - (b + 1) * size))) for b in range(count)
    ]
    return jnp.pad(jnp.concatenate(rows, axis=0), ((0, padded - count * size), (0, 0)))


def after(value, *others):
    return lax.optimization_barrier((value, *others))[0]


def row_major(x):
    return with_layout_constraint(x, Layout(major_to_minor=tuple(range(x.ndim))))


def gather_features(x):
    return lax.all_gather(x, "tp", axis=1, tiled=True)


def scatter_features(x):
    return lax.psum_scatter(x.astype(BF16), "tp", scatter_dimension=1, tiled=True).astype(F32)


def on_device(
    hidden_in, segment_ids, first_gain, input_weight, gelu_weight, conv_weight, conv_bias,
    recur_gate, input_gate, recur_bias, input_bias, decay_param, output_weight, second_gain,
    gate_weight, up_weight, down_weight, grad_out,
):
    tokens, share = hidden_in.shape
    channels = input_weight.shape[1]
    padded = -(-channels // 128) * 128
    extra = padded - channels
    taps = conv_weight.shape[0]
    halo = taps - 1
    blocks, size = recur_gate.shape[0], recur_gate.shape[1]
    width = grad_out.shape[1]
    units = gate_weight.shape[1]
    seq_devices = lax.axis_size("seq")
    tp_devices = lax.axis_size("tp")
    seq_place = lax.axis_index("seq")
    share_start = lax.axis_index("tp") * share
    order_a, order_b = bit_orders()

    route_a, route_b = [0, *order_a], [0, *order_b]

    x_low = side_by_side(hidden_in)
    full = gather_features(x_low)

    down_t = down_weight.T
    lead = down_t.shape[0]
    cut = lead // 2
    legs = [
        (jnp.concatenate([gate_weight, down_t[:cut]]), order_a),
        (jnp.concatenate([up_weight, down_t[cut:]]), order_b),
    ]
    first = [joined(a, order[:-1]) for a, order in legs]
    (
        segment_ids, input_weight, gelu_weight, recur_gate, input_gate, output_weight, grad_out,
        *first,
    ) = lax.optimization_barrier(
        (segment_ids, input_weight, gelu_weight, recur_gate, input_gate, output_weight, grad_out, *first)
    )
    second = [across(a, order[-1]) for a, (_, order) in zip(first, legs)]
    part = channels // seq_devices
    own_rows = lax.dynamic_slice_in_dim(output_weight, seq_place * part, part, 0)

    ids = segment_ids.astype(F32)
    prev_ids = shifted(ids[tokens - halo :], "seq", 1)
    prev_ids = jnp.where(seq_place == 0, -1.0, prev_ids)
    next_id = jnp.where(seq_place == seq_devices - 1, -1.0, shifted(ids[:1], "seq", -1))
    ext = jnp.concatenate([prev_ids, ids])
    same = [(ext[halo - k : halo - k + tokens] == ids).astype(F32) for k in range(taps)]
    masks = side_by_side(jnp.stack(same + [jnp.zeros_like(ids)] * (8 - taps), axis=1))
    next_ids = jnp.concatenate([ids[1:], next_id])
    closing = (next_ids != ids).astype(F32)[None, :]
    member = (segment_ids[None, :] == jnp.arange(SEGS, dtype=jnp.int32)[:, None]).astype(F32)
    picks = side_by_side((member * closing).T).T

    slope = -DECAY_SCALE * jax.nn.softplus(-decay_param)
    params = jnp.concatenate(
        [jnp.stack([conv_bias]), conv_weight, jnp.stack([recur_bias, input_bias, slope])], axis=0
    )
    params = jnp.pad(params, ((0, 0), (0, extra)))
    gates = jnp.concatenate(
        [block_diagonal(recur_gate, padded), block_diagonal(input_gate, padded)], axis=1
    )
    pad_rows = lambda a: jnp.pad(a, ((0, extra), (0, 0)))
    input_padded, gelu_padded = pad_rows(input_weight.T), pad_rows(gelu_weight.T)
    branch_weight = jnp.concatenate([input_padded, gelu_padded], axis=0)
    output_padded = pad_rows(output_weight)
    grad_rows = side_by_side(grad_out)
    (
        params, gates, branch_weight, output_padded, grad_rows, masks, own_rows, full,
        input_padded, gelu_padded,
    ) = lax.optimization_barrier(
        (
            params, gates, branch_weight, output_padded, grad_rows, masks, own_rows, full,
            input_padded, gelu_padded,
        )
    )

    x = full.astype(F32)
    r1 = lax.rsqrt(jnp.mean(x * x, axis=1, keepdims=True) + EPSILON)
    n1 = (x * r1 * first_gain).astype(BF16)
    both = row_major(contract_last(n1, branch_weight))
    last = both[tokens - 8 * halo :, :padded].reshape(halo, 8, padded)
    before = shifted(last[:, 7], "seq", 1)
    prev = jnp.concatenate([before[:, None], last[:, :7]], axis=1).reshape(8 * halo, padded)
    over_tp = lax.all_gather(own_rows, "tp", axis=0, tiled=True)
    conv, low, r, i, local, reach = forward_recurrence(both, prev, masks, params, gates)
    ends = jnp.stack([reach[tokens - 8 :], local[tokens - 8 :]])
    ends, over_tp, *second = lax.optimization_barrier((ends, over_tp, *second))
    ends = lax.all_gather(ends, "seq", axis=0)
    incoming = chained(ends[:, 0], ends[:, 1], seq_place, False)
    steps = lambda a: a.reshape(tokens // 8, 8, padded)
    state = (steps(local) + steps(reach) * incoming[None]).reshape(tokens, padded)
    mixed = (gelu(both[:, padded : padded + channels]) * state[:, :channels]).astype(BF16)
    mixed_full = lax.all_gather(mixed, "tp", axis=1, tiled=True)
    over_tp, _ = lax.optimization_barrier((over_tp, mixed))
    over_tp = over_tp.reshape(tp_devices, part, width)
    middle = width // 2
    rows_a = joined(over_tp[:, :, :middle], order_a)
    rows_b = joined(over_tp[:, :, middle:], order_b)
    grad_rows, *held = lax.optimization_barrier((grad_rows, *first, *second, mixed))
    own_a, own_b = (
        jnp.concatenate([held[leg], held[leg + len(legs)]]) for leg in range(len(legs))
    )
    tables = places([0, *order_a[::-1]]), places([0, *order_b[::-1]])
    gate_full, up_full, down_full = mlp_weights(
        own_a, across(own_a, 0), own_b, across(own_b, 0), tables, lead
    )
    d_hid = dot(grad_rows, down_full)
    output_full = output_rows(rows_a, across(rows_a, 0), rows_b, across(rows_b, 0), tables)
    d_hid, output_full, gate_full, up_full = lax.optimization_barrier(
        (d_hid, output_full, gate_full, up_full)
    )
    resid = x + dot(mixed_full, output_full)

    r2 = lax.rsqrt(jnp.mean(resid * resid, axis=1, keepdims=True) + EPSILON)
    n2 = (resid * r2 * second_gain).astype(BF16)
    resid_share = lax.dynamic_slice_in_dim(resid, share_start, share, 1)
    n2, resid_share = lax.optimization_barrier((n2, resid_share))
    hid, d_gate, d_up, pull2 = mlp_units(n2, gate_full, up_full, d_hid)
    d_n2_part = (contract_last(d_gate, gate_full) + contract_last(d_up, up_full)).astype(BF16)
    d_n2 = scatter_features(d_n2_part)
    n2_w, hid_w, pull2 = lax.optimization_barrier((n2, hid, pull2, d_n2_part))[:3]
    pull2 = lax.psum(jnp.sum(pull2, axis=1), "tp")
    grad_w = after(grad_rows, d_n2_part)
    grad_a, grad_b = relative(grad_w, route_a), relative(grad_w, route_b)
    half = units // 2
    n2_a, n2_b = relative(n2_w, route_a), relative(n2_w, route_b)
    products = [
        (n2_a, d_gate, order_a), (n2_b, d_up, order_b),
        (grad_a, hid_w[:, :half], order_a), (grad_b, hid_w[:, half:], order_b),
    ]
    middle = width // 2
    gives = [across(contract_first(l[:, middle:], r).astype(BF16), 0) for l, r, _ in products]
    sums2 = [
        contract_first(l[:, :middle], r) + give.astype(F32)
        for (l, r, _), give in zip(products, gives)
    ]
    d_n2, pull2, *sums2 = lax.optimization_barrier((d_n2, pull2, *sums2))
    pull2 = pull2[:, None]
    gain_share = lax.dynamic_slice_in_dim(second_gain, share_start, share)
    scaled = d_n2 * gain_share * r2
    scaled_low = scaled.astype(BF16)
    scaled_full = gather_features(scaled_low)
    hid_w, state_w, d_n2_w, n1_w, _, *sums2 = lax.optimization_barrier(
        (hid_w, state, d_n2, n1, scaled_low, *sums2)
    )
    n1_a, n1_b = relative(n1_w, route_a), relative(n1_w, route_b)
    finals = jnp.dot(picks, state_w, precision=lax.Precision.HIGHEST, preferred_element_type=F32)
    grad_second = jnp.sum(d_n2_w * resid_share * r2, axis=0)
    mlp = contract_last(hid_w, down_full).astype(BF16)
    for leg in range(len(order_a) - 1):
        sums2 = [crossed(v, order[leg], 0) for v, (_, _, order) in zip(sums2, products)]
    centre = r2 * r2 * pull2 * (1.0 / width)
    last_gives = [v[v.shape[0] // 2 :].astype(BF16) for v in sums2]
    kept2 = [v[: v.shape[0] // 2] for v in sums2]
    scaled_full, mlp, finals, grad_second, n1_a, n1_b, *last_gives = lax.optimization_barrier(
        (scaled_full, mlp, finals, grad_second, n1_a, n1_b, *last_gives)
    )
    mlp_sum = lax.psum_scatter(mlp, "tp", scatter_dimension=1, tiled=True)
    last_gives = [across(v, order[-1]) for v, (_, _, order) in zip(last_gives, products)]

    d_resid_low, grad_local, reach_back, dby, heads = reverse_recurrence(
        grad_rows, scaled_full, n2, r2 * pull2 * (1.0 / width), (1.0 / second_gain)[None],
        output_padded, both, r, state, masks, params,
    )
    back = lambda l, r: contract_first(l, r[:, middle:]).astype(BF16)
    front = lambda l, r: contract_first(l, r[:, :middle])

    def split(totals):
        half = totals[0].shape[1] // 2
        return [t[:, :half] for t in totals], [t[:, half:].astype(BF16) for t in totals]

    def sent(gives, orders, n):
        return [across(give, order[n]) for give, order in zip(gives, orders)]

    def met(keeps, fars):
        return [keep + far.astype(F32) for keep, far in zip(keeps, fars)]

    def returned(totals, orders, n):
        return [
            jnp.concatenate([t, across(t, order[n])], axis=1) for t, order in zip(totals, orders)
        ]

    orders = [order_a, order_b]
    last = len(order_a) - 1
    resid_a = relative(d_resid_low, route_a)
    gives = [back(mixed, resid_a), back(dby, n1_b)]
    heads, gives, last_gives = lax.optimization_barrier((heads, gives, last_gives))
    fars = [across(give, 0) for give in gives]
    outgoing = lax.all_gather(heads.reshape(2, 8, padded), "seq", axis=0)
    message = chained(outgoing[:, 1], outgoing[:, 0], seq_place, True)
    border = jnp.concatenate([incoming, message])
    keeps, gives = split(met([front(mixed, resid_a), front(dby, n1_b)], fars))
    border, gives, keeps = lax.optimization_barrier((border, gives, keeps))
    fars = sent(gives, orders, 0)
    d_main, tail, edge, sums, pair = gate_gradients(
        grad_local, reach_back, r, i, conv, state, both, masks, prev, border, params, gates
    )
    edge, fars, keeps = lax.optimization_barrier((edge, fars, keeps))
    beyond = shifted(edge.reshape(halo, 8, padded)[:, 0], "seq", -1)
    early = met(keeps, fars)
    for n in range(1, last):
        keeps, gives = split(early)
        early = met(keeps, sent(gives, orders, n))
    keeps, gives = split(early)
    fars = sent(gives, orders, last)
    dbx = settled(d_main, tail, edge, beyond)
    part_a = padded // 2
    gives = [back(dbx[:, :part_a], n1_a), back(dbx[:, part_a:], n1_b)]
    gives, dbx, fars = lax.optimization_barrier((gives, dbx, fars))
    far_in = [across(give, 0) for give in gives]
    early = [t.astype(BF16) for t in met(keeps, fars)]
    dbx, early = lax.optimization_barrier((dbx, early))
    early = returned(early, orders, last)
    d_n1_part = pair_product(dbx, dby, input_padded, gelu_padded)
    d_n1_part, mlp_sum = lax.optimization_barrier((d_n1_part, mlp_sum))
    d_n1 = scatter_features(d_n1_part)
    dbx, d_n1_w, early = lax.optimization_barrier((dbx, d_n1_part, early))
    for n in range(last - 1, -1, -1):
        early = returned(early, orders, n)
    early_parts = [(t, across(t, 0)) for t in early]

    totals = [front(dbx[:, :part_a], n1_a), front(dbx[:, part_a:], n1_b)]
    keeps, gives = split(met(totals, far_in))
    gives, pair, sums, d_n1_w = lax.optimization_barrier((gives, pair, sums, d_n1_w))
    totals = met(keeps, sent(gives, orders, 0))
    for n in range(1, last + 1):
        keeps, gives = split(totals)
        totals = met(keeps, sent(gives, orders, n))
    ready = totals = [t.astype(BF16) for t in totals]
    for n in range(last, 0, -1):
        totals = returned(totals, orders, n)
    far_in = sent(totals, orders, 0)
    near_in = totals

    first_part = jnp.sum(d_n1_w.astype(F32) * n1.astype(F32), axis=0) / first_gain
    pull1 = jnp.sum(d_n1_w.astype(F32) * n1.astype(F32), axis=1)
    second_part = lax.dynamic_update_slice(jnp.zeros((width,), F32), grad_second, (share_start,))
    over_tp = exchanged(jnp.concatenate([pull1, first_part, second_part]), "tp")
    pull1, gains = over_tp[:tokens, None], over_tp[tokens:]
    gate_grads = contract_first(low, pair)
    corner = lambda n, b: gate_grads[
        b * size : (b + 1) * size, n * padded + b * size : n * padded + (b + 1) * size
    ]
    corners = jnp.concatenate([corner(n, b) for b in range(blocks) for n in (0, 1)], axis=1)
    corners = jnp.pad(corners, ((0, 0), (0, width - corners.shape[1])))
    sums = jnp.sum(sums.reshape(8, 8, padded), axis=1)
    small = jnp.concatenate([sums, finals], axis=0)[:, :channels]
    packed = jnp.concatenate([gains, small.reshape(-1)])
    packed = jnp.pad(packed, (0, -packed.size % (8 * width))).reshape(-1, width)
    few = packed.shape[0]
    extras = [relative(jnp.concatenate([corners, packed]), route_b)]
    keeps, gives = split(extras)
    extras = met(keeps, [across(gives[0], 0)])
    for n in range(last + 1):
        keeps, gives = split(extras)
        extras = met(keeps, sent(gives, [order_b], n))
    extras = [t.astype(BF16) for t in extras]

    kept2, last_gives, mlp_sum, resid_out = lax.optimization_barrier(
        (kept2, last_gives, mlp_sum, resid_share, gives)
    )[:4]
    d_n1, resid_share = lax.optimization_barrier((d_n1, resid_share, ready))[:2]
    done2 = [v + give.astype(F32) for v, give in zip(kept2, last_gives)]
    grad_gate_weight, grad_up_weight = done2[:2]
    grad_down_weight = jnp.concatenate(done2[2:], axis=1).T
    g_share = lax.dynamic_slice_in_dim(grad_rows, share_start, share, 1).astype(F32)
    d_resid_share = g_share + scaled - resid_share * centre
    block_out = in_order((resid_out + mlp_sum.astype(F32)).astype(BF16))
    gain1_share = lax.dynamic_slice_in_dim(first_gain, share_start, share)
    grad_in = (
        d_resid_share
        + d_n1 * gain1_share * r1
        - x_low.astype(F32) * (r1 * r1 * pull1 * (1.0 / width))
    )
    grad_in = in_order(grad_in.astype(BF16))
    outputs = (block_out, grad_gate_weight, grad_up_weight, grad_down_weight)
    for n in range(last, -1, -1):
        extras = returned(extras, [order_b], n)
    extra_parts = [(t, across(t, 0)) for t in extras]
    tables = places(route_a), places(route_b)
    early_grads = ordered(
        early_parts, tables, [[(0, 0, channels)], [(1, 0, channels)]], "early_gradients"
    )
    far_in, outputs, early_grads = lax.optimization_barrier((far_in, outputs, early_grads))
    grad_output_weight, grad_gelu = early_grads
    totals = [jnp.concatenate(both_ways, axis=1) for both_ways in zip(near_in, far_in)]
    far_in = [across(t, 0) for t in totals]
    far_in, extra_parts, grad_in = lax.optimization_barrier((far_in, extra_parts, grad_in))
    in_parts = list(zip(totals, far_in))
    block_out, grad_gate_weight, grad_up_weight, grad_down_weight = outputs
    grad_input, corners, packed = ordered(
        in_parts + extra_parts,
        (*tables, tables[1]),
        [[(0, 0, part_a), (1, 0, channels - part_a)], [(2, 0, size)], [(2, size, few)]],
        "last_gradients",
    )
    packed = packed.reshape(-1)
    gains = packed[: 2 * width]
    small = packed[2 * width : 2 * width + small.size].reshape(small.shape)
    corner_of = lambda n: jnp.stack(
        [corners[:, (2 * b + n) * size : (2 * b + n + 1) * size] for b in range(blocks)]
    )
    grad_decay = small[2] * (DECAY_SCALE * jax.nn.sigmoid(-decay_param))
    return (
        block_out,
        grad_in,
        gains[:width],
        grad_input.T,
        grad_gelu.T,
        small[4:8],
        small[3],
        corner_of(0),
        corner_of(1),
        small[0],
        small[1],
        grad_decay,
        grad_output_weight,
        gains[width:],
        grad_gate_weight,
        grad_up_weight,
        grad_down_weight,
        small[8:],
    )


def solution(mesh):
    row = P("tp")
    return jax.shard_map(
        on_device,
        mesh=mesh,
        in_specs=(
            P("seq", "tp"), P("seq"), P(), P(None, "tp"), P(None, "tp"), P(None, "tp"), row,
            P("tp", None, None), P("tp", None, None), row, row, row, P("tp", None), P(),
            P("seq", "tp"), P("seq", "tp"), P("tp", "seq"), P("seq", None),
        ),
        out_specs=(
            P("seq", "tp"), P("seq", "tp"), P(), P(None, "tp"), P(None, "tp"), P(None, "tp"), row,
            P("tp", None, None), P("tp", None, None), row, row, row, P("tp", None), P(),
            P("seq", "tp"), P("seq", "tp"), P("tp", "seq"), P(None, "tp"),
        ),
        check_vma=False,
    )
```
